256 devices in a mesh: blk: 64 (over z, y, x_lo), feat: 4 (over x_hi, core).
Axes of the slice: x: 4 (x_hi: 2, x_lo: 2; x = x_hi * 2 + x_lo), y: 4, z: 8, core: 2. Of those that a mesh axis runs over, the one named last changes fastest.
Arguments:
- x_t: bfloat16 [256, 262144], P('feat', 'blk'), may hold values from -6 to 6
- weight: bfloat16 [256, 256], P('feat'), may hold values from -0.375 to 0.375
- cotangent: bfloat16 [256, 262144], P('feat', 'blk'), may hold values from -6 to 6
- tile_row: int32 [18432], P('blk'), may hold values from 0 to 31
- tile_col: int32 [18432], P('blk'), may hold values from 0 to 31
- tile_off: int32 [18432], P('blk'), may hold values from -4 to 4, as said below
- tile_vals: bfloat16 [18432, 128, 128], P('blk'), may hold values from -0.625 to 0.625
- tile_count: int32 [64], P('blk'), may hold values from 72 to 288, as said below
Outputs:
- out_t: bfloat16 [256, 262144], P('feat', 'blk')
- grad_x_t: bfloat16 [256, 262144], P('feat', 'blk')
- grad_weight: float32 [256, 256], P('feat')
The draws below stay inside these ranges and needn't reach their ends.
Inputs may be any that keep to these rules, and one draw needn't show every extreme that they name: `tile_off`: slots 0 to 8 of every partition name each offset once; slots may repeat a tile position, and repeated tiles add. `tile_count`: some partition lists 288 live tiles and some 288 // 4.
All inputs are finite; a program needn't handle non-finite values.
Results may differ from the reference program's by a relative error of at most 0.0062.
Values may be sent and summed in bfloat16 or wider, within the bound.
No kernel may reach another device: no remote copies, remote signals or barrier semaphores. Data moves between devices by JAX's collectives and lax.ppermute only.
A program may use at most 128 MiB of HBM per device.

```python
import math
import jax
import jax.numpy as jnp
from jax import lax

H = 256
TILE = 128
REACH = 4
TP = 32
MAXT = 288
NODES = 262144
N_BLK = 64


def draw_tile_row(key, part):
    return jax.random.randint(key, (N_BLK * MAXT,), 0, TP, dtype=jnp.int32)


def draw_tile_col(key, part):
    return jax.random.randint(jax.random.fold_in(key, 11), (N_BLK * MAXT,), 0, TP, dtype=jnp.int32)


def draw_tile_off(key, part):
    base = jax.random.fold_in(key, 23)
    keys = jax.random.split(base, N_BLK)
    firsts = jax.vmap(lambda single: jax.random.permutation(single, 2 * REACH + 1))(keys).astype(jnp.int32) - REACH
    others = jax.random.randint(jax.random.fold_in(base, 1), (N_BLK, MAXT - 2 * REACH - 1), -REACH, REACH + 1, dtype=jnp.int32)
    return jnp.concatenate([firsts, others], axis=1).reshape(N_BLK * MAXT)


def draw_tile_count(key, part):
    base = jax.random.fold_in(key, 37)
    shifts = jax.random.randint(base, (N_BLK,), 0, 3, dtype=jnp.int32)
    counts = jnp.right_shift(jnp.full((N_BLK,), MAXT, jnp.int32), shifts)
    busiest = jax.random.randint(jax.random.fold_in(base, 1), (), 0, N_BLK, dtype=jnp.int32)
    lightest = (busiest + 1 + jax.random.randint(jax.random.fold_in(base, 2), (), 0, N_BLK - 1, dtype=jnp.int32)) % N_BLK
    counts = counts.at[busiest].set(MAXT)
    counts = counts.at[lightest].set(MAXT // 4)
    return counts.astype(jnp.int32)


def steps_of(rng, extent, shards, smallest, top_value):
    factor_of = 1.0
    for position, blocks in shards:
        heights = jax.random.uniform(jax.random.fold_in(jax.random.fold_in(rng, 6), position), (blocks,), jnp.float32, smallest / len(shards), top_value / len(shards))
        factor_of = factor_of * jnp.repeat(jnp.exp(heights), extent[position] // blocks).reshape((-1,) + (1,) * (len(extent) - 1 - position))
    return factor_of


def normal_values(own_key, extent, width, limit, cuts=(), held_as=jnp.bfloat16):
    loudness = steps_of(own_key, extent, cuts, -0.22, 0.18) if cuts else 1.0
    drawn = jax.random.normal(own_key, extent, jnp.float32) * width * loudness
    return jnp.minimum(jnp.maximum(drawn, -limit), limit).astype(held_as)


def setup_inputs(seed: int = 0) -> dict:
    key_list = jax.random.split(jax.random.key(seed), 9)
    return {
        "x_t": normal_values(key_list[0], (H, NODES), 1.0, 6.0, ((0, 4), (1, 64))),
        "weight": normal_values(key_list[1], (H, H), H ** -0.5, 0.375, ((0, 4),)),
        "cotangent": normal_values(key_list[2], (H, NODES), 1.0, 6.0, ((0, 4), (1, 64))),
        "tile_row": draw_tile_row(jax.random.fold_in(key_list[8], 71), 0),
        "tile_col": draw_tile_col(jax.random.fold_in(key_list[8], 71), 0),
        "tile_off": draw_tile_off(jax.random.fold_in(key_list[8], 71), 0),
        "tile_vals": normal_values(key_list[6], (N_BLK * MAXT, TILE, TILE), ((4 * TILE) ** -0.5), 0.625, ((0, 64),)),
        "tile_count": draw_tile_count(jax.random.fold_in(key_list[8], 71), 0),
    }


def silu_slope(value):
    sig = jax.nn.sigmoid(value)
    return sig * (1.0 + value * (1.0 - sig))

def reference(x_t, weight, cotangent, tile_row, tile_col, tile_off, tile_vals, tile_count):
    parts = N_BLK
    proj_t = jnp.dot(weight.T, x_t, preferred_element_type=jnp.float32).astype(jnp.bfloat16)
    proj_b = proj_t.reshape(H, parts, TP, TILE)
    rows = tile_row.reshape(parts, MAXT)
    cols = tile_col.reshape(parts, MAXT)
    offs = tile_off.reshape(parts, MAXT)
    vals = tile_vals.reshape(parts, MAXT, TILE, TILE)
    slot_ids = jnp.arange(MAXT, dtype=jnp.int32)
    live = (slot_ids[None, :] < tile_count[:, None]).astype(jnp.float32)
    tile_ids = jnp.arange(TP, dtype=jnp.int32)

    def forward_block(part):
        source = ((part + offs[part]) % parts).astype(jnp.int32)
        pieces = proj_b[:, source, cols[part], :].astype(jnp.float32)
        prod = jnp.einsum('hsk,srk->hsr', pieces, vals[part].astype(jnp.float32), precision=lax.Precision.HIGHEST)
        row_hot = (rows[part][:, None] == tile_ids[None, :]).astype(jnp.float32) * live[part][:, None]
        return jnp.einsum('hsr,st->htr', prod, row_hot, precision=lax.Precision.HIGHEST)
    blocks = lax.map(forward_block, jnp.arange(parts, dtype=jnp.int32))
    pre_t = blocks.transpose(1, 0, 2, 3).reshape(H, NODES)
    out_t = jax.nn.silu(pre_t).astype(jnp.bfloat16)
    grad_pre = (cotangent.astype(jnp.float32) * silu_slope(pre_t)).astype(jnp.bfloat16)
    grad_b = grad_pre.reshape(H, parts, TP, TILE)

    def backward_step(total, part):
        own = lax.dynamic_index_in_dim(grad_b, part, 1, keepdims=False)
        pieces = jnp.take(own, rows[part], axis=1).astype(jnp.float32)
        contrib = jnp.einsum('hsr,srk->hsk', pieces, vals[part].astype(jnp.float32), precision=lax.Precision.HIGHEST)
        contrib = contrib * live[part][None, :, None]
        source = ((part + offs[part]) % parts).astype(jnp.int32)
        target = (source * TP + cols[part]).astype(jnp.int32)
        total = total.at[target].add(contrib.transpose(1, 0, 2))
        return (total, None)
    start = jnp.zeros((parts * TP, H, TILE), jnp.float32)
    total, unused = lax.scan(backward_step, start, jnp.arange(parts, dtype=jnp.int32))
    grad_proj = total.reshape(parts, TP, H, TILE).transpose(2, 0, 1, 3).reshape(H, NODES).astype(jnp.bfloat16)
    grad_weight = jnp.dot(x_t, grad_proj.T, preferred_element_type=jnp.float32) * (1.0 / math.sqrt(NODES))
    grad_x_t = jnp.dot(weight, grad_proj, preferred_element_type=jnp.float32).astype(jnp.bfloat16)
    return (out_t, grad_x_t, grad_weight)
```

```python
import functools
import math

import jax
import jax.numpy as jnp
from jax import lax
from jax.experimental import pallas as pl
from jax.experimental.pallas import tpu as pltpu
from jax.sharding import PartitionSpec as P

REACH = 4
SPAN = 2 * REACH + 1
UNROLL = 4
RING = 16
OFFSETS = [0] + [s * d for d in range(1, REACH + 1) for s in (1, -1)]


def shifted(block, distance):
    count = lax.axis_size("blk")
    route = [((i - distance) % count, i) for i in range(count)]
    return lax.ppermute(block, "blk", route)


def flipped(block, axis, bit):
    return lax.ppermute(block, axis, [(i, i ^ bit) for i in range(lax.axis_size(axis))])


def exchanged_columns(array, place):
    q = array.shape[1] // 4
    b = [array[:, i * q : (i + 1) * q] for i in range(4)]
    swapped = jnp.concatenate([b[1], b[0], b[3], b[2]], axis=1)
    array = jnp.where(place % 2 == 1, swapped, array)
    halves = jnp.concatenate([array[:, 2 * q :], array[:, : 2 * q]], axis=1)
    return jnp.where(place // 2 == 1, halves, array)


def plan_body(row_ref, col_ref, off_ref, count_ref, order_ref, src_ref, dst_ref, start_ref, fill):
    live = count_ref[0]

    def key_of(s):
        o = off_ref[s]
        return 2 * jnp.abs(o) - (o > 0).astype(jnp.int32)

    for k in range(16):
        fill[k] = 0

    def tally(s, c):
        k = key_of(s)
        fill[k] = fill[k] + 1
        return c

    lax.fori_loop(0, live, tally, 0)
    total = jnp.int32(0)
    for k in range(16):
        n = fill[k]
        start_ref[k] = total
        fill[k] = total
        total = total + n

    def place(s, c):
        k = key_of(s)
        at = fill[k]
        fill[k] = at + 1
        order_ref[at] = s
        src_ref[at] = k * 32 + col_ref[s]
        dst_ref[at] = row_ref[s]
        return c

    lax.fori_loop(0, live, place, 0)


def plan(tile_row, tile_col, tile_off, tile_count):
    slots = tile_row.shape[0]
    smem = pl.BlockSpec(memory_space=pltpu.SMEM)
    ints = jax.ShapeDtypeStruct((slots,), jnp.int32)
    return pl.pallas_call(
        plan_body,
        out_shape=(ints, ints, ints, jax.ShapeDtypeStruct((16,), jnp.int32)),
        in_specs=[smem] * 4,
        out_specs=(smem,) * 4,
        scratch_shapes=[pltpu.SMEM((16,), jnp.int32)],
        name="plan",
    )(tile_row, tile_col, tile_off, tile_count)


def tile_loop(begin, end, order_ref, vals_ref, ring, sems, multiply):
    n = end - begin

    def copy(i):
        slot = lax.rem(i, RING)
        return pltpu.make_async_copy(vals_ref.at[order_ref[begin + i]], ring.at[slot], sems.at[slot])

    def prime(i, c):
        copy(i).start()
        return c

    lax.fori_loop(0, jnp.minimum(n, RING), prime, 0)

    def step(first, width):
        for u in range(width):
            copy(first + u).wait()
        base = lax.rem(first, RING)
        multiply([begin + first + u for u in range(width)], [ring[base + u] for u in range(width)])
        for u in range(width):
            nxt = first + u + RING

            @pl.when(nxt < n)
            def _():
                copy(nxt).start()

    groups = n // UNROLL

    def group(g, c):
        step(g * UNROLL, UNROLL)
        return c

    lax.fori_loop(0, groups, group, 0)

    def single(i, c):
        step(i, 1)
        return c

    lax.fori_loop(groups * UNROLL, n, single, 0)


def forward_body(first, last, seeded, narrow, *refs):
    order_ref, src_ref, dst_ref, start_ref, vals_ref = refs[:5]
    slabs = refs[5 : 5 + last - first]
    rest = refs[5 + last - first :]
    if seeded:
        seed_ref, rest = rest[0], rest[1:]
    out_ref, acc, held, ring, sems, slab_sems = rest
    copies = [
        pltpu.make_async_copy(slab, held.at[j], slab_sems.at[j]) for j, slab in enumerate(slabs)
    ]
    for c in copies:
        c.start()
    if seeded:
        acc[...] = seed_ref[...]
    else:
        acc[...] = jnp.zeros_like(acc)
    for c in copies:
        c.wait()

    def multiply(positions, tiles):
        parts = []
        for at, tile in zip(positions, tiles):
            src = src_ref[at]
            lane = pl.multiple_of((src % 32) * 128, 128)
            piece = held[src // 32 - first, :, pl.ds(lane, 128)]
            parts.append(
                lax.dot_general(
                    piece, tile, (((1,), (1,)), ((), ())), preferred_element_type=jnp.float32
                )
            )
        for at, part in zip(positions, parts):
            lane = pl.multiple_of(dst_ref[at] * 128, 128)
            acc[:, pl.ds(lane, 128)] += part

    tile_loop(start_ref[first], start_ref[last], order_ref, vals_ref, ring, sems, multiply)
    out_ref[...] = acc[...].astype(out_ref.dtype)


def forward(first, last, listed, vals, slabs, seed, dtype):
    feats, nodes = slabs[0].shape
    smem = pl.BlockSpec(memory_space=pltpu.SMEM)
    hbm = pl.BlockSpec(memory_space=pl.ANY)
    vmem = pl.BlockSpec(memory_space=pltpu.VMEM)
    n = last - first
    return pl.pallas_call(
        functools.partial(forward_body, first, last, seed is not None, dtype),
        out_shape=jax.ShapeDtypeStruct((feats, nodes), dtype),
        in_specs=[smem] * 4 + [hbm] * (1 + n) + ([vmem] if seed is not None else []),
        out_specs=vmem,
        scratch_shapes=[
            pltpu.VMEM((feats, nodes), jnp.float32),
            pltpu.VMEM((n, feats, nodes), slabs[0].dtype),
            pltpu.VMEM((RING, 128, 128), vals.dtype),
            pltpu.SemaphoreType.DMA((RING,)),
            pltpu.SemaphoreType.DMA((n,)),
        ],
        name=f"forward_{first}_{last}",
    )(*listed, vals, *slabs, *(() if seed is None else (seed,)))


def backward_body(first, last, *refs):
    order_ref, src_ref, dst_ref, start_ref, vals_ref, grad_ref = refs[:6]
    outs = refs[6 : 6 + last - first]
    acc, ring, sems = refs[6 + last - first :]
    acc[...] = jnp.zeros_like(acc)

    def multiply(positions, tiles):
        parts = []
        for at, tile in zip(positions, tiles):
            lane = pl.multiple_of(dst_ref[at] * 128, 128)
            piece = grad_ref[:, pl.ds(lane, 128)]
            parts.append(jnp.dot(piece, tile, preferred_element_type=jnp.float32))
        for at, part in zip(positions, parts):
            src = src_ref[at]
            lane = pl.multiple_of((src % 32) * 128, 128)
            acc[src // 32 - first, :, pl.ds(lane, 128)] += part

    tile_loop(start_ref[first], start_ref[last], order_ref, vals_ref, ring, sems, multiply)
    for j, out in enumerate(outs):
        out[...] = acc[j].astype(out.dtype)


def backward(first, last, listed, vals, grad, dtypes):
    feats, nodes = grad.shape
    smem = pl.BlockSpec(memory_space=pltpu.SMEM)
    hbm = pl.BlockSpec(memory_space=pl.ANY)
    vmem = pl.BlockSpec(memory_space=pltpu.VMEM)
    n = last - first
    return pl.pallas_call(
        functools.partial(backward_body, first, last),
        out_shape=tuple(jax.ShapeDtypeStruct((feats, nodes), d) for d in dtypes),
        in_specs=[smem] * 4 + [hbm, vmem],
        out_specs=(vmem,) * n,
        scratch_shapes=[
            pltpu.VMEM((n, feats, nodes), jnp.float32),
            pltpu.VMEM((RING, 128, 128), vals.dtype),
            pltpu.SemaphoreType.DMA((RING,)),
        ],
        name=f"backward_{first}_{last}",
    )(*listed, vals, grad)


def middle_body(*refs):
    ys, cots, ws = refs[0:4], refs[4:8], refs[8:12]
    out_ref, grad_ref, wgrad_ref, turned = refs[12:]
    step = pl.program_id(0)
    feats = ys[0].shape[0]

    @pl.when(step == 0)
    def _():
        rows = []
        for k in range(4):
            w = ws[k][...]
            rows.append(
                jnp.concatenate(
                    [w[:, (j ^ k) * feats : ((j ^ k) + 1) * feats] for j in range(4)], axis=1
                )
            )
        turned[...] = jnp.concatenate(rows, axis=0).T
        wgrad_ref[...] = jnp.zeros_like(wgrad_ref)

    y = jnp.concatenate([r[...] for r in ys], axis=0)
    pre = jnp.dot(turned[...], y, preferred_element_type=jnp.float32)
    sig = jax.nn.sigmoid(pre)
    out_ref[...] = (pre[:feats] * sig[:feats]).astype(out_ref.dtype)
    cot = jnp.concatenate([r[...] for r in cots], axis=0).astype(jnp.float32)
    grad_pre = (cot * (sig * (1.0 + pre * (1.0 - sig)))).astype(jnp.bfloat16)
    grad_ref[...] = jnp.dot(
        ws[0][...], grad_pre, preferred_element_type=jnp.float32
    ).astype(grad_ref.dtype)
    wgrad_ref[...] += lax.dot_general(
        ys[0][...], grad_pre, (((1,), (1,)), ((), ())), preferred_element_type=jnp.float32
    )


def middle(ys, packed):
    feats, nodes = ys[0].shape
    hidden = 4 * feats
    chunk = 512
    piece = pl.BlockSpec((feats, chunk), lambda i: (0, i))
    w_spec = pl.BlockSpec((feats, hidden), lambda i: (0, nodes // hidden))
    whole = pl.BlockSpec((feats, hidden), lambda i: (0, 0))
    return pl.pallas_call(
        middle_body,
        grid=(nodes // chunk,),
        out_shape=(
            jax.ShapeDtypeStruct((feats, nodes), jnp.bfloat16),
            jax.ShapeDtypeStruct((feats, nodes), jnp.bfloat16),
            jax.ShapeDtypeStruct((feats, hidden), jnp.float32),
        ),
        in_specs=[piece] * 8 + [w_spec] * 4,
        out_specs=(piece, piece, whole),
        scratch_shapes=[pltpu.VMEM((hidden, hidden), jnp.bfloat16)],
        name="middle",
    )(*ys, *packed, *packed)


def per_device(x_t, weight, cotangent, tile_row, tile_col, tile_off, tile_vals, tile_count):
    nodes = x_t.shape[1]
    place = lax.axis_index("feat")
    slabs = {o: (shifted(x_t, -o) if o else x_t) for o in OFFSETS}
    own = jnp.concatenate([cotangent, exchanged_columns(weight, place)], axis=1)
    far = flipped(own, "feat", 2)
    packed = [own, flipped(own, "feat", 1), far, flipped(far, "feat", 1)]
    listed = plan(tile_row, tile_col, tile_off, tile_count)
    near = forward(0, 5, listed, tile_vals, [slabs[o] for o in OFFSETS[:5]], None, jnp.float32)
    y = forward(5, 9, listed, tile_vals, [slabs[o] for o in OFFSETS[5:]], near, jnp.bfloat16)
    y_far = flipped(y, "feat", 2)
    ys = [y, flipped(y, "feat", 1), y_far, flipped(y_far, "feat", 1)]
    out_t, grad, wgrad = middle(ys, packed)
    bf16 = jnp.bfloat16
    sent = dict(zip(OFFSETS[5:], backward(5, 9, listed, tile_vals, grad, [bf16] * 4)))
    total, *nearer = backward(0, 5, listed, tile_vals, grad, [jnp.float32] + [bf16] * 4)
    sent.update(zip(OFFSETS[1:5], nearer))
    for o in OFFSETS[::-1][:-1]:
        total = total + shifted(sent[o], o).astype(jnp.float32)
    wgrad = wgrad * (1.0 / math.sqrt(nodes * lax.axis_size("blk")))
    bit = 1
    while bit < lax.axis_size("blk"):
        wgrad = wgrad + flipped(wgrad, "blk", bit)
        bit *= 2
    return (out_t, total.astype(bf16), exchanged_columns(wgrad, place))


def solution(mesh):
    placed = (
        P("feat", "blk"),
        P("feat", None),
        P("feat", "blk"),
        P("blk"),
        P("blk"),
        P("blk"),
        P("blk", None, None),
        P("blk"),
    )
    return jax.shard_map(
        per_device,
        mesh=mesh,
        in_specs=placed,
        out_specs=(P("feat", "blk"), P("feat", "blk"), P("feat", None)),
        check_vma=False,
    )
```

```python
import functools
import math

import jax
import jax.numpy as jnp
from jax import lax
from jax.experimental import pallas as pl
from jax.experimental.pallas import tpu as pltpu
from jax.sharding import PartitionSpec as P

REACH = 4
SPAN = 2 * REACH + 1
UNROLL = 4
RING = 16
OFFSETS = [0, 1, 2, -2, 4, -4, -1, 3, -3]


def stepped(block, forth):
    count = lax.axis_size("blk")
    route = [((i + (2 if forth == (i % 2 == 0) else -2)) % count, i) for i in range(count)]
    return lax.ppermute(block, "blk", route)


def flipped(block, axis, bit):
    return lax.ppermute(block, axis, [(i, i ^ bit) for i in range(lax.axis_size(axis))])


def exchanged_columns(array, place):
    q = array.shape[1] // 4
    b = [array[:, i * q : (i + 1) * q] for i in range(4)]
    swapped = jnp.concatenate([b[1], b[0], b[3], b[2]], axis=1)
    array = jnp.where(place % 2 == 1, swapped, array)
    halves = jnp.concatenate([array[:, 2 * q :], array[:, : 2 * q]], axis=1)
    return jnp.where(place // 2 == 1, halves, array)


def plan_body(
    row_ref, col_ref, off_ref, count_ref, sign_ref, order_ref, src_ref, dst_ref, start_ref, fill, keys
):
    live = count_ref[0]
    sign = sign_ref[0]

    def key_of(s):
        return keys[off_ref[s] * sign + REACH]

    for k in range(16):
        fill[k] = 0
    for k, offset in enumerate(OFFSETS):
        keys[offset + REACH] = k

    def tally(s, c):
        k = key_of(s)
        fill[k] = fill[k] + 1
        return c

    lax.fori_loop(0, live, tally, 0)
    total = jnp.int32(0)
    for k in range(16):
        n = fill[k]
        start_ref[k] = total
        fill[k] = total
        total = total + n

    def place(s, c):
        k = key_of(s)
        at = fill[k]
        fill[k] = at + 1
        order_ref[at] = s
        src_ref[at] = k * 32 + col_ref[s]
        dst_ref[at] = row_ref[s]
        return c

    lax.fori_loop(0, live, place, 0)


def plan(tile_row, tile_col, tile_off, tile_count, sign):
    slots = tile_row.shape[0]
    smem = pl.BlockSpec(memory_space=pltpu.SMEM)
    ints = jax.ShapeDtypeStruct((slots,), jnp.int32)
    return pl.pallas_call(
        plan_body,
        out_shape=(ints, ints, ints, jax.ShapeDtypeStruct((16,), jnp.int32)),
        in_specs=[smem] * 5,
        out_specs=(smem,) * 4,
        scratch_shapes=[pltpu.SMEM((16,), jnp.int32)] * 2,
        name="plan",
    )(tile_row, tile_col, tile_off, tile_count, sign)


def tile_loop(begin, end, order_ref, vals_ref, ring, sems, multiply):
    n = end - begin

    def copy(i):
        slot = lax.rem(i, RING)
        return pltpu.make_async_copy(vals_ref.at[order_ref[begin + i]], ring.at[slot], sems.at[slot])

    def prime(i, c):
        copy(i).start()
        return c

    lax.fori_loop(0, jnp.minimum(n, RING), prime, 0)

    def step(first, width):
        for u in range(width):
            copy(first + u).wait()
        base = lax.rem(first, RING)
        multiply([begin + first + u for u in range(width)], [ring[base + u] for u in range(width)])
        for u in range(width):
            nxt = first + u + RING

            @pl.when(nxt < n)
            def _():
                copy(nxt).start()

    groups = n // UNROLL

    def group(g, c):
        step(g * UNROLL, UNROLL)
        return c

    lax.fori_loop(0, groups, group, 0)

    def single(i, c):
        step(i, 1)
        return c

    lax.fori_loop(groups * UNROLL, n, single, 0)


def forward_body(first, last, seeded, narrow, *refs):
    order_ref, src_ref, dst_ref, start_ref, vals_ref = refs[:5]
    slabs = refs[5 : 5 + last - first]
    rest = refs[5 + last - first :]
    if seeded:
        seed_ref, rest = rest[0], rest[1:]
    out_ref, acc, held, ring, sems, slab_sems = rest
    copies = [
        pltpu.make_async_copy(slab, held.at[j], slab_sems.at[j]) for j, slab in enumerate(slabs)
    ]
    for c in copies:
        c.start()
    if seeded:
        acc[...] = seed_ref[...]
    else:
        acc[...] = jnp.zeros_like(acc)
    for c in copies:
        c.wait()

    def multiply(positions, tiles):
        parts = []
        for at, tile in zip(positions, tiles):
            src = src_ref[at]
            lane = pl.multiple_of((src % 32) * 128, 128)
            piece = held[src // 32 - first, :, pl.ds(lane, 128)]
            parts.append(
                lax.dot_general(
                    piece, tile, (((1,), (1,)), ((), ())), preferred_element_type=jnp.float32
                )
            )
        for at, part in zip(positions, parts):
            lane = pl.multiple_of(dst_ref[at] * 128, 128)
            acc[:, pl.ds(lane, 128)] += part

    tile_loop(start_ref[first], start_ref[last], order_ref, vals_ref, ring, sems, multiply)
    out_ref[...] = acc[...].astype(out_ref.dtype)


def forward(first, last, listed, vals, slabs, seed, dtype):
    feats, nodes = slabs[0].shape
    smem = pl.BlockSpec(memory_space=pltpu.SMEM)
    hbm = pl.BlockSpec(memory_space=pl.ANY)
    vmem = pl.BlockSpec(memory_space=pltpu.VMEM)
    n = last - first
    return pl.pallas_call(
        functools.partial(forward_body, first, last, seed is not None, dtype),
        out_shape=jax.ShapeDtypeStruct((feats, nodes), dtype),
        in_specs=[smem] * 4 + [hbm] * (1 + n) + ([vmem] if seed is not None else []),
        out_specs=vmem,
        scratch_shapes=[
            pltpu.VMEM((feats, nodes), jnp.float32),
            pltpu.VMEM((n, feats, nodes), slabs[0].dtype),
            pltpu.VMEM((RING, 128, 128), vals.dtype),
            pltpu.SemaphoreType.DMA((RING,)),
            pltpu.SemaphoreType.DMA((n,)),
        ],
        name=f"forward_{first}_{last}",
    )(*listed, vals, *slabs, *(() if seed is None else (seed,)))


def backward_body(first, last, *refs):
    order_ref, src_ref, dst_ref, start_ref, vals_ref, grad_ref = refs[:6]
    outs = refs[6 : 6 + last - first]
    acc, ring, sems = refs[6 + last - first :]
    acc[...] = jnp.zeros_like(acc)

    def multiply(positions, tiles):
        parts = []
        for at, tile in zip(positions, tiles):
            lane = pl.multiple_of(dst_ref[at] * 128, 128)
            piece = grad_ref[:, pl.ds(lane, 128)]
            parts.append(jnp.dot(piece, tile, preferred_element_type=jnp.float32))
        for at, part in zip(positions, parts):
            src = src_ref[at]
            lane = pl.multiple_of((src % 32) * 128, 128)
            acc[src // 32 - first, :, pl.ds(lane, 128)] += part

    tile_loop(start_ref[first], start_ref[last], order_ref, vals_ref, ring, sems, multiply)
    for j, out in enumerate(outs):
        out[...] = acc[j].astype(out.dtype)


def backward(first, last, listed, vals, grad, dtypes):
    feats, nodes = grad.shape
    smem = pl.BlockSpec(memory_space=pltpu.SMEM)
    hbm = pl.BlockSpec(memory_space=pl.ANY)
    vmem = pl.BlockSpec(memory_space=pltpu.VMEM)
    n = last - first
    return pl.pallas_call(
        functools.partial(backward_body, first, last),
        out_shape=tuple(jax.ShapeDtypeStruct((feats, nodes), d) for d in dtypes),
        in_specs=[smem] * 4 + [hbm, vmem],
        out_specs=(vmem,) * n,
        scratch_shapes=[
            pltpu.VMEM((n, feats, nodes), jnp.float32),
            pltpu.VMEM((RING, 128, 128), vals.dtype),
            pltpu.SemaphoreType.DMA((RING,)),
        ],
        name=f"backward_{first}_{last}",
    )(*listed, vals, grad)


def middle_body(*refs):
    ys, cots, ws = refs[0:4], refs[4:8], refs[8:12]
    out_ref, grad_ref, wgrad_ref, turned = refs[12:]
    step = pl.program_id(0)
    feats = ys[0].shape[0]

    @pl.when(step == 0)
    def _():
        rows = []
        for k in range(4):
            w = ws[k][...]
            rows.append(
                jnp.concatenate(
                    [w[:, (j ^ k) * feats : ((j ^ k) + 1) * feats] for j in range(4)], axis=1
                )
            )
        turned[...] = jnp.concatenate(rows, axis=0).T
        wgrad_ref[...] = jnp.zeros_like(wgrad_ref)

    y = jnp.concatenate([r[...] for r in ys], axis=0)
    pre = jnp.dot(turned[...], y, preferred_element_type=jnp.float32)
    sig = jax.nn.sigmoid(pre)
    out_ref[...] = (pre[:feats] * sig[:feats]).astype(out_ref.dtype)
    cot = jnp.concatenate([r[...] for r in cots], axis=0).astype(jnp.float32)
    grad_pre = (cot * (sig * (1.0 + pre * (1.0 - sig)))).astype(jnp.bfloat16)
    grad_ref[...] = jnp.dot(
        ws[0][...], grad_pre, preferred_element_type=jnp.float32
    ).astype(grad_ref.dtype)
    wgrad_ref[...] += lax.dot_general(
        ys[0][...], grad_pre, (((1,), (1,)), ((), ())), preferred_element_type=jnp.float32
    )


def middle(ys, packed):
    feats, nodes = ys[0].shape
    hidden = 4 * feats
    chunk = 512
    piece = pl.BlockSpec((feats, chunk), lambda i: (0, i))
    w_spec = pl.BlockSpec((feats, hidden), lambda i: (0, nodes // hidden))
    whole = pl.BlockSpec((feats, hidden), lambda i: (0, 0))
    return pl.pallas_call(
        middle_body,
        grid=(nodes // chunk,),
        out_shape=(
            jax.ShapeDtypeStruct((feats, nodes), jnp.bfloat16),
            jax.ShapeDtypeStruct((feats, nodes), jnp.bfloat16),
            jax.ShapeDtypeStruct((feats, hidden), jnp.float32),
        ),
        in_specs=[piece] * 8 + [w_spec] * 4,
        out_specs=(piece, piece, whole),
        scratch_shapes=[pltpu.VMEM((hidden, hidden), jnp.bfloat16)],
        name="middle",
    )(*ys, *packed, *packed)


def fenced(*groups):
    return lax.optimization_barrier(groups)


def summed(value, radix_bits):
    low, high = radix_bits
    return [flipped(value, "blk", low), flipped(value, "blk", high), flipped(value, "blk", low | high)]


def per_device(x_t, weight, cotangent, tile_row, tile_col, tile_off, tile_vals, tile_count):
    nodes = x_t.shape[1]
    f32, bf16 = jnp.float32, jnp.bfloat16
    place = lax.axis_index("feat")
    sign = (1 - 2 * (lax.axis_index("blk") % 2)).astype(jnp.int32).reshape(1)
    own = jnp.concatenate([cotangent, exchanged_columns(weight, place)], axis=1)

    x, u, v = flipped(x_t, "blk", 1), stepped(x_t, True), stepped(x_t, False)
    listed = plan(tile_row, tile_col, tile_off, tile_count, sign)
    x, u, v, listed, own = fenced(x, u, v, listed, own)
    m, n, ux = stepped(u, True), stepped(v, False), flipped(u, "blk", 1)
    y = forward(0, 4, listed, tile_vals, [x_t, x, u, v], None, f32)
    m, n, ux, y, x, own = fenced(m, n, ux, y, x, own)
    xu, mx = stepped(x, True), flipped(m, "blk", 1)
    far = flipped(own, "feat", 2)
    y = forward(4, 7, listed, tile_vals, [m, n, ux], y, f32)
    xu, mx, y = fenced(xu, mx, y)
    y = forward(7, 9, listed, tile_vals, [xu, mx], y, bf16)

    packed = [own, flipped(own, "feat", 1), far, flipped(far, "feat", 1)]
    y_far = flipped(y, "feat", 2)
    ys = [y, flipped(y, "feat", 1), y_far, flipped(y_far, "feat", 1)]
    out_t, grad, wgrad = middle(ys, packed)
    wgrad = wgrad * (1.0 / math.sqrt(nodes * lax.axis_size("blk")))

    to_xu, to_mx = backward(7, 9, listed, tile_vals, grad, [bf16] * 2)
    from_xu, from_mx = stepped(to_xu, False), flipped(to_mx, "blk", 1)
    parts = summed(wgrad, (1, 2))
    to_m, to_n, to_ux = backward(4, 7, listed, tile_vals, grad, [f32, bf16, bf16])
    from_xu, from_mx, to_m, to_n, to_ux, parts, grad = fenced(
        from_xu, from_mx, to_m, to_n, to_ux, parts, grad
    )
    from_m = stepped((to_m + from_mx.astype(f32)).astype(bf16), False)
    from_n, from_ux = stepped(to_n, True), flipped(to_ux, "blk", 1)
    wgrad = (wgrad + parts[0]) + (parts[1] + parts[2])
    parts = summed(wgrad, (4, 8))
    total, to_x, to_u, to_v = backward(0, 4, listed, tile_vals, grad, [f32] * 4)
    from_m, from_n, from_ux, total, to_x, to_u, to_v, parts = fenced(
        from_m, from_n, from_ux, total, to_x, to_u, to_v, parts
    )
    wgrad = (wgrad + parts[0]) + (parts[1] + parts[2])
    from_u = stepped((to_u + from_m.astype(f32) + from_ux.astype(f32)).astype(bf16), False)
    from_v = stepped((to_v + from_n.astype(f32)).astype(bf16), True)
    from_x = flipped((to_x + from_xu.astype(f32)).astype(bf16), "blk", 1)
    parts = summed(wgrad, (16, 32))
    wgrad = (wgrad + parts[0]) + (parts[1] + parts[2])
    total = total + from_u.astype(f32) + from_v.astype(f32) + from_x.astype(f32)
    return (out_t, total.astype(bf16), exchanged_columns(wgrad, place))


def solution(mesh):
    placed = (
        P("feat", "blk"),
        P("feat", None),
        P("feat", "blk"),
        P("blk"),
        P("blk"),
        P("blk"),
        P("blk", None, None),
        P("blk"),
    )
    return jax.shard_map(
        per_device,
        mesh=mesh,
        in_specs=placed,
        out_specs=(P("feat", "blk"), P("feat", "blk"), P("feat", None)),
        check_vma=False,
    )
```

```python
import functools
import math

import jax
import jax.numpy as jnp
from jax import lax
from jax.experimental import pallas as pl
from jax.experimental.pallas import tpu as pltpu
from jax.sharding import PartitionSpec as P

REACH = 4
GROUP = 8
DEPTH = 4
WAVES = [[0, 1, 2, -2], [4, -4, -1], [3, -3]]
HALF = 16
BUCKETS = 4
KEYS = [len(WAVES[0]), len(WAVES[1]), len(WAVES[2]), len(WAVES[2])]


def stepped(block, forth):
    count = lax.axis_size("blk")
    route = [((i + (2 if forth == (i % 2 == 0) else -2)) % count, i) for i in range(count)]
    return lax.ppermute(block, "blk", route)


def flipped(block, axis, bit):
    return lax.ppermute(block, axis, [(i, i ^ bit) for i in range(lax.axis_size(axis))])


def exchanged_columns(array, place):
    q = array.shape[1] // 4
    b = [array[:, i * q : (i + 1) * q] for i in range(4)]
    swapped = jnp.concatenate([b[1], b[0], b[3], b[2]], axis=1)
    array = jnp.where(place % 2 == 1, swapped, array)
    halves = jnp.concatenate([array[:, 2 * q :], array[:, : 2 * q]], axis=1)
    return jnp.where(place // 2 == 1, halves, array)


COST = pl.CostEstimate(flops=0, transcendentals=0, bytes_accessed=24_000_000)


def plan_body(cap, row_ref, col_ref, off_ref, count_ref, sign_ref, list_ref, fill, home):
    sign = sign_ref[0]
    for k in range(BUCKETS):
        fill[k] = 0
    for w, wave in enumerate(WAVES):
        for j, offset in enumerate(wave):
            home[offset + REACH] = w + 16 * j

    def place(s, c):
        row = row_ref[s]
        at_home = home[off_ref[s] * sign + REACH]
        wave = at_home & 15
        bucket = wave + (row >> 4) * (wave >> 1)
        n = fill[bucket]
        fill[bucket] = n + 1
        list_ref[bucket * cap + n] = (
            s + (row << 9) + (col_ref[s] << 15) + ((at_home >> 4) << 20)
        )
        return c

    lax.fori_loop(0, count_ref[0], place, 0)
    for k in range(BUCKETS):
        n = fill[k]
        groups = (n + GROUP - 1) >> 3

        def pad(i, c):
            list_ref[k * cap + i] = 32 << 9
            return c

        lax.fori_loop(n, groups * GROUP, pad, 0)
        list_ref[BUCKETS * cap + k] = groups


def plan(tile_row, tile_col, tile_off, tile_count, sign):
    cap = tile_row.shape[0] + GROUP
    smem = pl.BlockSpec(memory_space=pltpu.SMEM)
    return pl.pallas_call(
        functools.partial(plan_body, cap),
        out_shape=jax.ShapeDtypeStruct((BUCKETS * cap + 16,), jnp.int32),
        in_specs=[smem] * 5,
        out_specs=smem,
        scratch_shapes=[pltpu.SMEM((16,), jnp.int32)] * 2,
        cost_estimate=COST,
        name="plan",
    )(tile_row, tile_col, tile_off, tile_count, sign)


def tile_copies(bucket, list_ref, vals_ref, ring, sems):
    base = bucket * ((list_ref.shape[0] - 16) // BUCKETS)
    groups = list_ref[list_ref.shape[0] - 16 + bucket]

    def start(g):
        @pl.when(g < groups)
        def _():
            slot = g & (DEPTH - 1)
            for u in range(GROUP):
                entry = list_ref[base + g * GROUP + u]
                pltpu.make_async_copy(
                    vals_ref.at[entry & 511], ring.at[slot, u], sems.at[slot]
                ).start()

    def wait(g):
        slot = g & (DEPTH - 1)
        pltpu.make_async_copy(vals_ref.at[pl.ds(0, GROUP)], ring.at[slot], sems.at[slot]).wait()

    return base, groups, start, wait


def tile_loop(copies, list_ref, ring, multiply):
    base, groups, start, wait = copies

    def body(g, c):
        start(g + DEPTH - 1)
        wait(g)
        slot = g & (DEPTH - 1)
        multiply(
            [list_ref[base + g * GROUP + u] for u in range(GROUP)],
            [ring[slot, u] for u in range(GROUP)],
        )
        return c

    lax.fori_loop(0, groups, body, 0)


def column(tile):
    return pl.ds(pl.multiple_of(tile * 128, 128), 128)


def paired(first, second):
    zero = jnp.zeros_like(first)
    return jnp.concatenate(
        [jnp.concatenate([first, zero], axis=1), jnp.concatenate([zero, second], axis=1)], axis=0
    )


def forward_body(bucket, seeded, parts, *refs):
    n = KEYS[bucket]
    list_ref, vals_ref = refs[:2]
    slabs, rest = refs[2 : 2 + n], refs[2 + n :]
    if seeded:
        seed_ref, rest = rest[0], rest[1:]
    outs, (acc, held, ring, sems) = rest[:parts], rest[parts:]
    width = outs[0].shape[1]
    first_row = HALF if bucket == 3 else 0
    copies = tile_copies(bucket, list_ref, vals_ref, ring, sems)
    for g in range(DEPTH - 1):
        copies[2](g)
    if seeded:
        acc[:, : parts * width] = seed_ref[...]
    else:
        acc[...] = jnp.zeros_like(acc)
    for j, slab in enumerate(slabs):
        held[j] = slab[...]
    feats = acc.shape[0]

    def multiply(entries, tiles):
        products = []
        for u in range(0, GROUP, 2):
            p, q = [
                held[e >> 20, :, column((e >> 15) & 31)] for e in (entries[u], entries[u + 1])
            ]
            products.append(
                lax.dot_general(
                    paired(p, q),
                    jnp.concatenate([tiles[u], tiles[u + 1]], axis=1),
                    (((1,), (1,)), ((), ())),
                    preferred_element_type=jnp.float32,
                )
            )
        for u in range(GROUP):
            row = ((entries[u] >> 9) & 63) - first_row
            half = products[u // 2][u % 2 * feats : (u % 2 + 1) * feats]
            acc[:, column(row)] += half

    tile_loop(copies, list_ref, ring, multiply)
    for j, out in enumerate(outs):
        out[...] = acc[:, j * width : (j + 1) * width].astype(out.dtype)


def forward(bucket, listed, vals, slabs, seed, parts, dtype):
    feats, nodes = slabs[0].shape
    covered = nodes if bucket < 2 else HALF * 128
    wide = nodes + 128 if bucket != 3 else nodes + 128 - HALF * 128
    smem = pl.BlockSpec(memory_space=pltpu.SMEM)
    hbm = pl.BlockSpec(memory_space=pl.ANY)
    vmem = pl.BlockSpec(memory_space=pltpu.VMEM)
    return pl.pallas_call(
        functools.partial(forward_body, bucket, seed is not None, parts),
        out_shape=(jax.ShapeDtypeStruct((feats, covered // parts), dtype),) * parts,
        in_specs=[smem, hbm] + [vmem] * (len(slabs) + (seed is not None)),
        out_specs=(vmem,) * parts,
        scratch_shapes=[
            pltpu.VMEM((feats, wide), jnp.float32),
            pltpu.VMEM((len(slabs), feats, nodes), slabs[0].dtype),
            pltpu.VMEM((DEPTH, GROUP, 128, 128), vals.dtype),
            pltpu.SemaphoreType.DMA((DEPTH,)),
        ],
        cost_estimate=COST,
        name=f"forward_{bucket}",
    )(listed, vals, *slabs, *(() if seed is None else (seed,)))


def backward_body(bucket, seeded, *refs):
    n = KEYS[bucket]
    list_ref, vals_ref, grad_ref = refs[:3]
    rest = refs[3:]
    if seeded:
        seeds, rest = rest[:n], rest[n:]
    outs, (acc, ring, sems) = rest[:n], rest[n:]
    copies = tile_copies(bucket, list_ref, vals_ref, ring, sems)
    for g in range(DEPTH - 1):
        copies[2](g)
    for j in range(n):
        acc[j] = seeds[j][...] if seeded else jnp.zeros_like(acc[j])
    feats = acc.shape[1]

    def multiply(entries, tiles):
        products = []
        for u in range(0, GROUP, 2):
            p, q = [
                grad_ref[:, column((e >> 9) & 31)] for e in (entries[u], entries[u + 1])
            ]
            products.append(
                jnp.dot(
                    paired(p, q),
                    jnp.concatenate([tiles[u], tiles[u + 1]], axis=0),
                    preferred_element_type=jnp.float32,
                )
            )
        for u in range(GROUP):
            e = entries[u]
            half = products[u // 2][u % 2 * feats : (u % 2 + 1) * feats]
            acc[(e >> 20) + ((e >> 14) & 1) * n, :, column((e >> 15) & 31)] += half

    tile_loop(copies, list_ref, ring, multiply)
    for j, out in enumerate(outs):
        out[...] = acc[j].astype(out.dtype)


def backward(bucket, listed, vals, grad, seeds, dtypes):
    feats, nodes = grad.shape[0], 32 * 128
    smem = pl.BlockSpec(memory_space=pltpu.SMEM)
    hbm = pl.BlockSpec(memory_space=pl.ANY)
    vmem = pl.BlockSpec(memory_space=pltpu.VMEM)
    n = len(dtypes)
    return pl.pallas_call(
        functools.partial(backward_body, bucket, bool(seeds)),
        out_shape=tuple(jax.ShapeDtypeStruct((feats, nodes), d) for d in dtypes),
        in_specs=[smem, hbm] + [vmem] * (1 + len(seeds)),
        out_specs=(vmem,) * n,
        scratch_shapes=[
            pltpu.VMEM((n + 1, feats, nodes), jnp.float32),
            pltpu.VMEM((DEPTH, GROUP, 128, 128), vals.dtype),
            pltpu.SemaphoreType.DMA((DEPTH,)),
        ],
        cost_estimate=COST,
        name=f"backward_{bucket}",
    )(listed, vals, grad, *seeds)


def middle_body(half, *refs):
    ys, packed, refs = refs[0:4], refs[4:8], refs[8:]
    if half:
        (out_before, grad_before, wgrad_before), refs = refs[:3], refs[3:]
    out_ref, grad_ref, wgrad_ref = refs
    feats, nodes = ys[0].shape
    hidden = 4 * feats
    chunk = 512
    rows = []
    for k in range(4):
        w = packed[k][:, 2 * nodes :]
        rows.append(
            jnp.concatenate(
                [w[:, (j ^ k) * feats : ((j ^ k) + 1) * feats] for j in range(4)], axis=1
            )
        )
    own_rows = rows[0]
    turned = jnp.concatenate(rows, axis=0).T
    at = half * nodes
    wgrad = jnp.zeros((feats, hidden), jnp.float32)
    if half:
        out_ref[:, :nodes] = out_before[...]
        grad_ref[:, :nodes] = grad_before[...]
        wgrad = wgrad_before[...]
    for start in range(0, nodes, chunk):
        here = slice(start, start + chunk)
        there = slice(at + start, at + start + chunk)
        y = jnp.concatenate([r[:, here] for r in ys], axis=0)
        pre = jnp.dot(turned, y, preferred_element_type=jnp.float32)
        sig = jax.nn.sigmoid(pre)
        out_ref[:, there] = (pre[:feats] * sig[:feats]).astype(out_ref.dtype)
        cot = jnp.concatenate([r[:, there] for r in packed], axis=0).astype(jnp.float32)
        grad_pre = (cot * (sig * (1.0 + pre * (1.0 - sig)))).astype(jnp.bfloat16)
        grad_ref[:, there] = jnp.dot(
            own_rows, grad_pre, preferred_element_type=jnp.float32
        ).astype(grad_ref.dtype)
        wgrad += lax.dot_general(
            ys[0][:, here], grad_pre, (((1,), (1,)), ((), ())), preferred_element_type=jnp.float32
        )
    wgrad_ref[...] = wgrad


def middle(half, ys, packed, before):
    feats, nodes = ys[0].shape
    reached = (half + 1) * nodes
    vmem = pl.BlockSpec(memory_space=pltpu.VMEM)
    return pl.pallas_call(
        functools.partial(middle_body, half),
        out_shape=(
            jax.ShapeDtypeStruct((feats, reached), jnp.bfloat16),
            jax.ShapeDtypeStruct((feats, reached), jnp.bfloat16),
            jax.ShapeDtypeStruct((feats, 4 * feats), jnp.float32),
        ),
        in_specs=[vmem] * (8 + len(before)),
        out_specs=(vmem,) * 3,
        cost_estimate=COST,
        name=f"middle_{half}",
    )(*ys, *packed, *before)


def fenced(*groups):
    return lax.optimization_barrier(groups)


def summed(value, radix_bits):
    low, high = radix_bits
    return [flipped(value, "blk", low), flipped(value, "blk", high), flipped(value, "blk", low | high)]


def per_device(x_t, weight, cotangent, tile_row, tile_col, tile_off, tile_vals, tile_count):
    nodes = x_t.shape[1]
    f32, bf16 = jnp.float32, jnp.bfloat16
    place = lax.axis_index("feat")
    sign = (1 - 2 * (lax.axis_index("blk") % 2)).astype(jnp.int32).reshape(1)
    own = jnp.concatenate([cotangent, exchanged_columns(weight, place)], axis=1)

    x, u, v = flipped(x_t, "blk", 1), stepped(x_t, True), stepped(x_t, False)
    listed = plan(tile_row, tile_col, tile_off, tile_count, sign)
    x, u, v, listed, own = fenced(x, u, v, listed, own)
    m, n, ux = stepped(u, True), stepped(v, False), flipped(u, "blk", 1)
    (y,) = forward(0, listed, tile_vals, [x_t, x, u, v], None, 1, f32)
    m, n, ux, y, x, own = fenced(m, n, ux, y, x, own)
    xu, mx = stepped(x, True), flipped(m, "blk", 1)
    far = flipped(own, "feat", 2)
    y_a, y_b = forward(1, listed, tile_vals, [m, n, ux], y, 2, f32)
    xu, mx, y_a, y_b = fenced(xu, mx, y_a, y_b)

    (y_a,) = forward(2, listed, tile_vals, [xu, mx], y_a, 1, bf16)
    far_a = flipped(y_a, "feat", 2)
    _, own, far = fenced(y_a, own, far)
    packed = [own, flipped(own, "feat", 1), far, flipped(far, "feat", 1)]
    (y_b,) = forward(3, listed, tile_vals, [xu, mx], y_b, 1, bf16)
    far_a, y_b = fenced(far_a, y_b)
    ys_a = [y_a, flipped(y_a, "feat", 1), far_a, flipped(far_a, "feat", 1)]
    far_b, side_b = flipped(y_b, "feat", 2), flipped(y_b, "feat", 1)
    before = middle(0, ys_a, packed, ())
    begun = backward(2, listed, tile_vals, before[1], (), [f32] * 2)
    begun, far_b = fenced(begun, far_b)
    ys_b = [y_b, side_b, far_b, flipped(far_b, "feat", 1)]
    out_t, grad, wgrad = middle(1, ys_b, packed, before)
    wgrad = exchanged_columns(wgrad, place) * (1.0 / math.sqrt(nodes * lax.axis_size("blk")))
    parts = summed(wgrad, (1, 2))

    to_xu, to_mx = backward(3, listed, tile_vals, grad, begun, [bf16] * 2)
    from_xu, from_mx = stepped(to_xu, False), flipped(to_mx, "blk", 1)
    to_m, to_n, to_ux = backward(1, listed, tile_vals, grad, (), [f32, bf16, bf16])
    from_xu, from_mx, to_m, to_n, to_ux, parts, grad = fenced(
        from_xu, from_mx, to_m, to_n, to_ux, parts, grad
    )
    from_m = stepped((to_m + from_mx.astype(f32)).astype(bf16), False)
    from_n, from_ux = stepped(to_n, True), flipped(to_ux, "blk", 1)
    wgrad = (wgrad + parts[0]) + (parts[1] + parts[2])
    parts = summed(wgrad, (4, 8))
    total, to_x, to_u, to_v = backward(0, listed, tile_vals, grad, (), [f32] * 4)
    from_m, from_n, from_ux, total, to_x, to_u, to_v, parts = fenced(
        from_m, from_n, from_ux, total, to_x, to_u, to_v, parts
    )
    from_u = stepped((to_u + from_m.astype(f32) + from_ux.astype(f32)).astype(bf16), False)
    from_v = stepped((to_v + from_n.astype(f32)).astype(bf16), True)
    from_x = flipped((to_x + from_xu.astype(f32)).astype(bf16), "blk", 1)
    wgrad = (wgrad + parts[0]) + (parts[1] + parts[2])
    parts = summed(wgrad, (16, 32))
    wgrad = (wgrad + parts[0]) + (parts[1] + parts[2])
    total = total + from_u.astype(f32) + from_v.astype(f32) + from_x.astype(f32)
    return (out_t, total.astype(bf16), wgrad)


def solution(mesh):
    placed = (
        P("feat", "blk"),
        P("feat", None),
        P("feat", "blk"),
        P("blk"),
        P("blk"),
        P("blk"),
        P("blk", None, None),
        P("blk"),
    )
    return jax.shard_map(
        per_device,
        mesh=mesh,
        in_specs=placed,
        out_specs=(P("feat", "blk"), P("feat", "blk"), P("feat", None)),
        check_vma=False,
    )
```

```python
import functools
import math

import jax
import jax.numpy as jnp
from jax import lax
from jax.experimental import pallas as pl
from jax.experimental.pallas import tpu as pltpu
from jax.sharding import PartitionSpec as P

REACH = 4
GROUP = 8
WAVES = [[0, 1, 2, -2], [4, -4], [3, -1, -3]]
MIB = 1 << 20


def stepped(block, forth):
    count = lax.axis_size("blk")
    route = [((i + (2 if forth == (i % 2 == 0) else -2)) % count, i) for i in range(count)]
    return lax.ppermute(block, "blk", route)


def flipped(block, axis, bit):
    return lax.ppermute(block, axis, [(i, i ^ bit) for i in range(lax.axis_size(axis))])


def exchanged_columns(array, place):
    q = array.shape[1] // 4
    b = [array[:, i * q : (i + 1) * q] for i in range(4)]
    swapped = jnp.concatenate([b[1], b[0], b[3], b[2]], axis=1)
    array = jnp.where(place % 2 == 1, swapped, array)
    halves = jnp.concatenate([array[:, 2 * q :], array[:, : 2 * q]], axis=1)
    return jnp.where(place // 2 == 1, halves, array)


COST = pl.CostEstimate(flops=0, transcendentals=0, bytes_accessed=24_000_000)
SMEM = pl.BlockSpec(memory_space=pltpu.SMEM)
VMEM = pl.BlockSpec(memory_space=pltpu.VMEM)


def near(array):
    return pltpu.with_memory_space_constraint(array, pltpu.VMEM)


def kept(mib):
    return pltpu.CompilerParams(vmem_limit_bytes=mib * MIB)


def plan_body(cap, row_ref, col_ref, off_ref, count_ref, sign_ref, list_ref, fill, home):
    sign = sign_ref[0]
    for w, wave in enumerate(WAVES):
        fill[w] = 0
        for j, offset in enumerate(wave):
            home[offset + REACH] = w + 16 * j

    def place(s, c):
        at_home = home[off_ref[s] * sign + REACH]
        wave = at_home & 15
        n = fill[wave]
        fill[wave] = n + 1
        list_ref[wave * cap + n] = (
            s + (row_ref[s] << 9) + (col_ref[s] << 15) + ((at_home >> 4) << 20)
        )
        return c

    lax.fori_loop(0, count_ref[0], place, 0)
    for w in range(len(WAVES)):
        n = fill[w]
        groups = (n + GROUP - 1) >> 3

        def pad(i, c):
            list_ref[w * cap + i] = 32 << 9
            return c

        lax.fori_loop(n, groups * GROUP, pad, 0)
        list_ref[len(WAVES) * cap + w] = groups


def plan(tile_row, tile_col, tile_off, tile_count, sign):
    cap = tile_row.shape[0] + GROUP
    return pl.pallas_call(
        functools.partial(plan_body, cap),
        out_shape=jax.ShapeDtypeStruct((len(WAVES) * cap + 16,), jnp.int32),
        in_specs=[SMEM] * 5,
        out_specs=SMEM,
        scratch_shapes=[pltpu.SMEM((16,), jnp.int32)] * 2,
        cost_estimate=COST,
        compiler_params=kept(2),
        name="plan",
    )(tile_row, tile_col, tile_off, tile_count, sign)


def tile_loop(wave, list_ref, vals_ref, multiply):
    cap = (list_ref.shape[0] - 16) // len(WAVES)

    def body(g, c):
        entries = [list_ref[wave * cap + g * GROUP + u] for u in range(GROUP)]
        multiply(entries, [vals_ref[e & 511] for e in entries])
        return c

    lax.fori_loop(0, list_ref[len(WAVES) * cap + wave], body, 0)


def column(tile):
    return pl.ds(pl.multiple_of(tile * 128, 128), 128)


def paired(first, second):
    zero = jnp.zeros_like(first)
    return jnp.concatenate(
        [jnp.concatenate([first, zero], axis=1), jnp.concatenate([zero, second], axis=1)], axis=0
    )


def forward_body(wave, seeded, *refs):
    n = len(WAVES[wave])
    list_ref, vals_ref = refs[:2]
    slabs, rest = refs[2 : 2 + n], refs[2 + n :]
    if seeded:
        seed_ref, rest = rest[0], rest[1:]
    out_ref, held = rest[:2]
    acc = rest[2] if len(rest) > 2 else out_ref
    acc[...] = seed_ref[...] if seeded else jnp.zeros_like(acc)
    for j, slab in enumerate(slabs):
        held[j] = slab[...]
    feats = acc.shape[0]
    held[n, :, 0:128] = jnp.zeros((feats, 128), held.dtype)

    def multiply(entries, tiles):
        pieces = [
            held[(e >> 20) + ((e >> 14) & 1) * n, :, column((e >> 15) & 31)] for e in entries
        ]
        products = [
            lax.dot_general(
                paired(pieces[u], pieces[u + 1]),
                jnp.concatenate([tiles[u], tiles[u + 1]], axis=1),
                (((1,), (1,)), ((), ())),
                preferred_element_type=jnp.float32,
            )
            for u in range(0, GROUP, 2)
        ]
        for u, e in enumerate(entries):
            half = products[u // 2][u % 2 * feats : (u % 2 + 1) * feats]
            acc[:, column((e >> 9) & 31)] += half

    tile_loop(wave, list_ref, vals_ref, multiply)
    if acc is not out_ref:
        out_ref[...] = acc[...].astype(out_ref.dtype)


def forward(wave, listed, vals, slabs, seed, dtype):
    feats, nodes = slabs[0].shape
    wide = dtype == jnp.float32
    return pl.pallas_call(
        functools.partial(forward_body, wave, seed is not None),
        out_shape=pltpu.VMEM((feats, nodes), dtype),
        in_specs=[SMEM] + [VMEM] * (1 + len(slabs) + (seed is not None)),
        out_specs=VMEM,
        scratch_shapes=[pltpu.VMEM((len(slabs) + 1, feats, nodes), slabs[0].dtype)]
        + ([] if wide else [pltpu.VMEM((feats, nodes), jnp.float32)]),
        cost_estimate=COST,
        compiler_params=kept(8),
        name=f"forward_{wave}",
    )(listed, near(vals), *map(near, slabs), *(() if seed is None else (near(seed),)))


def backward_body(wave, *refs):
    n = len(WAVES[wave])
    list_ref, vals_ref, grad_ref = refs[:3]
    outs, acc = refs[3:-1], refs[-1]
    acc[0:n] = jnp.zeros((n,) + acc.shape[1:], acc.dtype)
    feats = acc.shape[1]

    def multiply(entries, tiles):
        pieces = [grad_ref[:, column((e >> 9) & 31)] for e in entries]
        products = [
            jnp.dot(
                paired(pieces[u], pieces[u + 1]),
                jnp.concatenate([tiles[u], tiles[u + 1]], axis=0),
                preferred_element_type=jnp.float32,
            )
            for u in range(0, GROUP, 2)
        ]
        for u, e in enumerate(entries):
            half = products[u // 2][u % 2 * feats : (u % 2 + 1) * feats]
            acc[(e >> 20) + ((e >> 14) & 1) * n, :, column((e >> 15) & 31)] += half

    tile_loop(wave, list_ref, vals_ref, multiply)
    for j, out in enumerate(outs):
        out[...] = acc[j].astype(out.dtype)


def backward(wave, listed, vals, grad, dtypes):
    n = len(dtypes)
    return pl.pallas_call(
        functools.partial(backward_body, wave),
        out_shape=tuple(pltpu.VMEM(grad.shape, d) for d in dtypes),
        in_specs=[SMEM, VMEM, VMEM],
        out_specs=(VMEM,) * n,
        scratch_shapes=[pltpu.VMEM((n + 1,) + grad.shape, jnp.float32)],
        cost_estimate=COST,
        compiler_params=kept(8),
        name=f"backward_{wave}",
    )(listed, near(vals), near(grad))


def middle_body(*refs):
    ys, packed, (out_ref, grad_ref, wgrad_ref) = refs[0:4], refs[4:8], refs[8:]
    feats, nodes = ys[0].shape
    hidden = 4 * feats
    chunk = 512
    rows = []
    for k in range(4):
        w = packed[k][:, nodes:]
        rows.append(
            jnp.concatenate(
                [w[:, (j ^ k) * feats : ((j ^ k) + 1) * feats] for j in range(4)], axis=1
            )
        )
    own_rows = rows[0]
    turned = jnp.concatenate(rows, axis=0).T
    wgrad = jnp.zeros((feats, hidden), jnp.float32)
    for start in range(0, nodes, chunk):
        here = slice(start, start + chunk)
        y = jnp.concatenate([r[:, here] for r in ys], axis=0)
        pre = jnp.dot(turned, y, preferred_element_type=jnp.float32)
        sig = jax.nn.sigmoid(pre)
        out_ref[:, here] = (pre[:feats] * sig[:feats]).astype(out_ref.dtype)
        cot = jnp.concatenate([r[:, here] for r in packed], axis=0).astype(jnp.float32)
        grad_pre = (cot * (sig * (1.0 + pre * (1.0 - sig)))).astype(jnp.bfloat16)
        grad_ref[:, here] = jnp.dot(
            own_rows, grad_pre, preferred_element_type=jnp.float32
        ).astype(grad_ref.dtype)
        wgrad += lax.dot_general(
            ys[0][:, here], grad_pre, (((1,), (1,)), ((), ())), preferred_element_type=jnp.float32
        )
    wgrad_ref[...] = wgrad


def middle(ys, packed):
    feats, nodes = ys[0].shape
    return pl.pallas_call(
        middle_body,
        out_shape=(
            jax.ShapeDtypeStruct((feats, nodes), jnp.bfloat16),
            pltpu.VMEM((feats, nodes), jnp.bfloat16),
            pltpu.VMEM((feats, 4 * feats), jnp.float32),
        ),
        in_specs=[VMEM] * 8,
        out_specs=(VMEM,) * 3,
        cost_estimate=COST,
        compiler_params=kept(10),
        name="middle",
    )(*map(near, ys), *map(near, packed))


def fenced(*groups):
    return lax.optimization_barrier(groups)


def summed(value, radix_bits):
    low, high = radix_bits
    return [flipped(value, "blk", low), flipped(value, "blk", high), flipped(value, "blk", low | high)]


def per_device(x_t, weight, cotangent, tile_row, tile_col, tile_off, tile_vals, tile_count):
    nodes = x_t.shape[1]
    f32, bf16 = jnp.float32, jnp.bfloat16
    place = lax.axis_index("feat")
    sign = (1 - 2 * (lax.axis_index("blk") % 2)).astype(jnp.int32).reshape(1)
    own = jnp.concatenate([cotangent, exchanged_columns(weight, place)], axis=1)

    x, u, v = flipped(x_t, "blk", 1), stepped(x_t, True), stepped(x_t, False)
    listed = plan(tile_row, tile_col, tile_off, tile_count, sign)
    x, u, v, listed, own = fenced(x, u, v, listed, own)
    m, n, far = stepped(u, True), stepped(v, False), flipped(own, "feat", 2)
    y = forward(0, listed, tile_vals, [x_t, x, u, v], None, f32)
    m, n, y, x = fenced(m, n, y, x)
    mx, xu, xv = flipped(m, "blk", 1), stepped(x, True), stepped(x, False)
    y = forward(1, listed, tile_vals, [m, n], y, f32)
    xu, xv, mx, y, far, own = fenced(xu, xv, mx, y, far, own)
    packed = [own, flipped(own, "feat", 1), far, flipped(far, "feat", 1)]
    y = forward(2, listed, tile_vals, [xu, xv, mx], y, bf16)
    y_far = flipped(y, "feat", 2)
    out_t, grad, wgrad = middle([y, flipped(y, "feat", 1), y_far, flipped(y_far, "feat", 1)], packed)

    to_xu, to_xv, to_mx = backward(2, listed, tile_vals, grad, [bf16] * 3)
    from_mx = flipped(to_mx, "blk", 1)
    from_xu, from_xv = stepped(to_xu, False), stepped(to_xv, True)
    to_m, to_n = backward(1, listed, tile_vals, grad, [f32, bf16])
    wgrad = exchanged_columns(wgrad, place) * (1.0 / math.sqrt(nodes * lax.axis_size("blk")))
    parts = summed(wgrad, (1, 2))
    from_mx, to_m, grad = fenced(from_mx, to_m, grad)
    from_m = stepped((to_m + from_mx.astype(f32)).astype(bf16), False)
    from_n = stepped(to_n, True)
    total, to_x, to_u, to_v = backward(0, listed, tile_vals, grad, [f32] * 4)
    wgrad, parts, to_x = fenced(wgrad, parts, to_x)
    wgrad = (wgrad + parts[0]) + (parts[1] + parts[2])
    parts = summed(wgrad, (4, 8))
    from_x = flipped((to_x + from_xu.astype(f32) + from_xv.astype(f32)).astype(bf16), "blk", 1)
    from_v = stepped((to_v + from_n.astype(f32)).astype(bf16), True)
    from_u = stepped((to_u + from_m.astype(f32)).astype(bf16), False)
    wgrad = (wgrad + parts[0]) + (parts[1] + parts[2])
    parts = summed(wgrad, (16, 32))
    wgrad = (wgrad + parts[0]) + (parts[1] + parts[2])
    total = total + from_u.astype(f32) + from_v.astype(f32) + from_x.astype(f32)
    return (out_t, total.astype(bf16), wgrad)


def solution(mesh):
    placed = (
        P("feat", "blk"),
        P("feat", None),
        P("feat", "blk"),
        P("blk"),
        P("blk"),
        P("blk"),
        P("blk", None, None),
        P("blk"),
    )
    return jax.shard_map(
        per_device,
        mesh=mesh,
        in_specs=placed,
        out_specs=(P("feat", "blk"), P("feat", "blk"), P("feat", None)),
        check_vma=False,
    )
```

```python
import functools
import math

import jax
import jax.numpy as jnp
from jax import lax
from jax.experimental import pallas as pl
from jax.experimental.pallas import tpu as pltpu
from jax.sharding import PartitionSpec as P

REACH = 4
GROUP = 8
WAVES = [[0, 1, 2, -2], [4, -4], [3, -1, -3]]
MIB = 1 << 20


def stepped(block, forth):
    count = lax.axis_size("blk")
    route = [((i + (2 if forth == (i % 2 == 0) else -2)) % count, i) for i in range(count)]
    return lax.ppermute(block, "blk", route)


def flipped(block, axis, bit):
    return lax.ppermute(block, axis, [(i, i ^ bit) for i in range(lax.axis_size(axis))])


def exchanged_columns(array, place):
    q = array.shape[1] // 4
    b = [array[:, i * q : (i + 1) * q] for i in range(4)]
    swapped = jnp.concatenate([b[1], b[0], b[3], b[2]], axis=1)
    array = jnp.where(place % 2 == 1, swapped, array)
    halves = jnp.concatenate([array[:, 2 * q :], array[:, : 2 * q]], axis=1)
    return jnp.where(place // 2 == 1, halves, array)


COST = pl.CostEstimate(flops=0, transcendentals=0, bytes_accessed=6_000_000)
SMEM = pl.BlockSpec(memory_space=pltpu.SMEM)
VMEM = pl.BlockSpec(memory_space=pltpu.VMEM)


def near(array):
    return pltpu.with_memory_space_constraint(array, pltpu.VMEM)


def kept(mib):
    return pltpu.CompilerParams(vmem_limit_bytes=mib * MIB)


def plan_body(cap, row_ref, col_ref, off_ref, count_ref, sign_ref, list_ref, fill, home):
    sign = sign_ref[0]
    for w, wave in enumerate(WAVES):
        fill[w] = 0
        for j, offset in enumerate(wave):
            home[offset + REACH] = w + 16 * j

    def place(s, c):
        at_home = home[off_ref[s] * sign + REACH]
        wave = at_home & 15
        n = fill[wave]
        fill[wave] = n + 1
        list_ref[wave * cap + n] = (
            s + (row_ref[s] << 9) + (col_ref[s] << 15) + ((at_home >> 4) << 20)
        )
        return c

    lax.fori_loop(0, count_ref[0], place, 0)
    for w in range(len(WAVES)):
        n = fill[w]
        groups = (n + GROUP - 1) >> 3

        def pad(i, c):
            list_ref[w * cap + i] = 32 << 9
            return c

        lax.fori_loop(n, groups * GROUP, pad, 0)
        list_ref[len(WAVES) * cap + w] = groups


def plan(tile_row, tile_col, tile_off, tile_count, sign):
    cap = tile_row.shape[0] + GROUP
    return pl.pallas_call(
        functools.partial(plan_body, cap),
        out_shape=jax.ShapeDtypeStruct((len(WAVES) * cap + 16,), jnp.int32),
        in_specs=[SMEM] * 5,
        out_specs=SMEM,
        scratch_shapes=[pltpu.SMEM((16,), jnp.int32)] * 2,
        cost_estimate=COST,
        compiler_params=kept(2),
        name="plan",
    )(tile_row, tile_col, tile_off, tile_count, sign)


def tile_loop(wave, list_ref, vals_ref, multiply):
    cap = (list_ref.shape[0] - 16) // len(WAVES)

    def body(g, c):
        entries = [list_ref[wave * cap + g * GROUP + u] for u in range(GROUP)]
        multiply(entries, [vals_ref[e & 511] for e in entries])
        return c

    lax.fori_loop(0, list_ref[len(WAVES) * cap + wave], body, 0)


def column(tile):
    return pl.ds(pl.multiple_of(tile * 128, 128), 128)


def paired(first, second):
    zero = jnp.zeros_like(first)
    return jnp.concatenate(
        [jnp.concatenate([first, zero], axis=1), jnp.concatenate([zero, second], axis=1)], axis=0
    )


def forward_body(wave, seeded, *refs):
    n = len(WAVES[wave])
    list_ref, vals_ref = refs[:2]
    slabs, rest = refs[2 : 2 + n], refs[2 + n :]
    if seeded:
        seed_ref, rest = rest[0], rest[1:]
    out_ref, held = rest[:2]
    acc = rest[2] if len(rest) > 2 else out_ref
    acc[...] = seed_ref[...] if seeded else jnp.zeros_like(acc)
    for j, slab in enumerate(slabs):
        held[j] = slab[...]
    feats = acc.shape[0]
    held[n, :, 0:128] = jnp.zeros((feats, 128), held.dtype)

    def multiply(entries, tiles):
        pieces = [
            held[(e >> 20) + ((e >> 14) & 1) * n, :, column((e >> 15) & 31)] for e in entries
        ]
        products = [
            lax.dot_general(
                paired(pieces[u], pieces[u + 1]),
                jnp.concatenate([tiles[u], tiles[u + 1]], axis=1),
                (((1,), (1,)), ((), ())),
                preferred_element_type=jnp.float32,
            )
            for u in range(0, GROUP, 2)
        ]
        for u, e in enumerate(entries):
            half = products[u // 2][u % 2 * feats : (u % 2 + 1) * feats]
            acc[:, column((e >> 9) & 31)] += half

    tile_loop(wave, list_ref, vals_ref, multiply)
    if acc is not out_ref:
        out_ref[...] = acc[...].astype(out_ref.dtype)


def forward(wave, listed, vals, slabs, seed, dtype):
    feats, nodes = slabs[0].shape
    wide = dtype == jnp.float32
    return pl.pallas_call(
        functools.partial(forward_body, wave, seed is not None),
        out_shape=pltpu.VMEM((feats, nodes), dtype),
        in_specs=[SMEM] + [VMEM] * (1 + len(slabs) + (seed is not None)),
        out_specs=VMEM,
        scratch_shapes=[pltpu.VMEM((len(slabs) + 1, feats, nodes), slabs[0].dtype)]
        + ([] if wide else [pltpu.VMEM((feats, nodes), jnp.float32)]),
        cost_estimate=COST,
        compiler_params=kept(8),
        name=f"forward_{wave}",
    )(listed, near(vals), *map(near, slabs), *(() if seed is None else (near(seed),)))


def backward_body(wave, *refs):
    n = len(WAVES[wave])
    list_ref, vals_ref, grad_ref = refs[:3]
    outs, acc = refs[3:-1], refs[-1]
    acc[0:n] = jnp.zeros((n,) + acc.shape[1:], acc.dtype)
    feats = acc.shape[1]

    def multiply(entries, tiles):
        pieces = [grad_ref[:, column((e >> 9) & 31)] for e in entries]
        products = [
            jnp.dot(
                paired(pieces[u], pieces[u + 1]),
                jnp.concatenate([tiles[u], tiles[u + 1]], axis=0),
                preferred_element_type=jnp.float32,
            )
            for u in range(0, GROUP, 2)
        ]
        for u, e in enumerate(entries):
            half = products[u // 2][u % 2 * feats : (u % 2 + 1) * feats]
            acc[(e >> 20) + ((e >> 14) & 1) * n, :, column((e >> 15) & 31)] += half

    tile_loop(wave, list_ref, vals_ref, multiply)
    for j, out in enumerate(outs):
        out[...] = acc[j].astype(out.dtype)


def backward(wave, listed, vals, grad, dtypes):
    n = len(dtypes)
    return pl.pallas_call(
        functools.partial(backward_body, wave),
        out_shape=tuple(pltpu.VMEM(grad.shape, d) for d in dtypes),
        in_specs=[SMEM, VMEM, VMEM],
        out_specs=(VMEM,) * n,
        scratch_shapes=[pltpu.VMEM((n + 1,) + grad.shape, jnp.float32)],
        cost_estimate=COST,
        compiler_params=kept(8),
        name=f"backward_{wave}",
    )(listed, near(vals), near(grad))


def middle_body(factor, place_ref, *refs):
    ys, packed, (out_ref, grad_ref, wgrad_ref) = refs[0:4], refs[4:8], refs[8:]
    feats, nodes = ys[0].shape
    hidden = 4 * feats
    chunk = 512
    rows = []
    for k in range(4):
        w = packed[k][:, nodes:]
        rows.append(
            jnp.concatenate(
                [w[:, (j ^ k) * feats : ((j ^ k) + 1) * feats] for j in range(4)], axis=1
            )
        )
    own_rows = rows[0]
    turned = jnp.concatenate(rows, axis=0).T
    wgrad = jnp.zeros((feats, hidden), jnp.float32)
    for start in range(0, nodes, chunk):
        here = slice(start, start + chunk)
        y = jnp.concatenate([r[:, here] for r in ys], axis=0)
        pre = jnp.dot(turned, y, preferred_element_type=jnp.float32)
        sig = jax.nn.sigmoid(pre)
        out_ref[:, here] = (pre[:feats] * sig[:feats]).astype(out_ref.dtype)
        cot = jnp.concatenate([r[:, here] for r in packed], axis=0).astype(jnp.float32)
        grad_pre = (cot * (sig * (1.0 + pre * (1.0 - sig)))).astype(jnp.bfloat16)
        grad_ref[:, here] = jnp.dot(
            own_rows, grad_pre, preferred_element_type=jnp.float32
        ).astype(grad_ref.dtype)
        wgrad += lax.dot_general(
            ys[0][:, here], grad_pre, (((1,), (1,)), ((), ())), preferred_element_type=jnp.float32
        )
    wgrad_ref[...] = exchanged_columns(wgrad, place_ref[0]) * factor


def middle(place, ys, packed):
    feats, nodes = ys[0].shape
    factor = 1.0 / math.sqrt(nodes * lax.axis_size("blk"))
    return pl.pallas_call(
        functools.partial(middle_body, factor),
        out_shape=(
            jax.ShapeDtypeStruct((feats, nodes), jnp.bfloat16),
            pltpu.VMEM((feats, nodes), jnp.bfloat16),
            pltpu.VMEM((feats, 4 * feats), jnp.float32),
        ),
        in_specs=[SMEM] + [VMEM] * 8,
        out_specs=(VMEM,) * 3,
        cost_estimate=COST,
        compiler_params=kept(10),
        name="middle",
    )(place.astype(jnp.int32).reshape(1), *map(near, ys), *map(near, packed))


def fenced(*groups):
    return lax.optimization_barrier(groups)


def per_device(x_t, weight, cotangent, tile_row, tile_col, tile_off, tile_vals, tile_count):
    nodes = x_t.shape[1]
    f32, bf16 = jnp.float32, jnp.bfloat16
    place = lax.axis_index("feat")
    sign = (1 - 2 * (lax.axis_index("blk") % 2)).astype(jnp.int32).reshape(1)
    own = jnp.concatenate([cotangent, exchanged_columns(weight, place)], axis=1)

    x, u, v = flipped(x_t, "blk", 1), stepped(x_t, True), stepped(x_t, False)
    listed = plan(tile_row, tile_col, tile_off, tile_count, sign)
    x, u, v, listed, own = fenced(x, u, v, listed, own)
    m, n, far = stepped(u, True), stepped(v, False), flipped(own, "feat", 2)
    y = forward(0, listed, tile_vals, [x_t, x, u, v], None, f32)
    m, n, y, x = fenced(m, n, y, x)
    mx, xu, xv = flipped(m, "blk", 1), stepped(x, True), stepped(x, False)
    y = forward(1, listed, tile_vals, [m, n], y, f32)
    xu, xv, mx, y, far, own = fenced(xu, xv, mx, y, far, own)
    packed = [own, flipped(own, "feat", 1), far, flipped(far, "feat", 1)]
    y = forward(2, listed, tile_vals, [xu, xv, mx], y, bf16)
    y_far = flipped(y, "feat", 2)
    ys = [y, flipped(y, "feat", 1), y_far, flipped(y_far, "feat", 1)]
    out_t, grad, wgrad = middle(place, ys, packed)

    part = flipped(wgrad, "blk", 2)
    to_xu, to_xv, to_mx = backward(2, listed, tile_vals, grad, [bf16] * 3)
    to_xu, to_xv, to_mx, part, grad = fenced(to_xu, to_xv, to_mx, part, grad)
    from_mx, from_xu, from_xv = flipped(to_mx, "blk", 1), stepped(to_xu, False), stepped(to_xv, True)
    wgrad = wgrad + part
    part = flipped(wgrad, "blk", 8)
    to_m, to_n = backward(1, listed, tile_vals, grad, [f32, bf16])
    part, to_m, grad = fenced(part, to_m, grad)
    wgrad = wgrad + part
    part = flipped(wgrad, "blk", 16)
    total, to_x, to_u, to_v = backward(0, listed, tile_vals, grad, [f32] * 4)
    from_mx, from_xu, from_xv, to_m, to_n, total, to_x, to_u, to_v, part = fenced(
        from_mx, from_xu, from_xv, to_m, to_n, total, to_x, to_u, to_v, part
    )
    from_m = stepped((to_m + from_mx.astype(f32)).astype(bf16), False)
    from_n = stepped(to_n, True)
    to_x = (to_x + from_xu.astype(f32) + from_xv.astype(f32)).astype(bf16)
    wgrad = wgrad + part
    wgrad = wgrad + flipped(wgrad, "blk", 32)
    wgrad = wgrad + flipped(wgrad, "blk", 1)
    from_m, from_n, to_x, to_u, to_v, wgrad = fenced(from_m, from_n, to_x, to_u, to_v, wgrad)
    part = flipped(wgrad, "blk", 4)
    from_u = stepped((to_u + from_m.astype(f32)).astype(bf16), False)
    from_v = stepped((to_v + from_n.astype(f32)).astype(bf16), True)
    from_x = flipped(to_x, "blk", 1)
    wgrad = wgrad + part
    total = total + from_u.astype(f32) + from_v.astype(f32) + from_x.astype(f32)
    return (out_t, total.astype(bf16), wgrad)


def solution(mesh):
    placed = (
        P("feat", "blk"),
        P("feat", None),
        P("feat", "blk"),
        P("blk"),
        P("blk"),
        P("blk"),
        P("blk", None, None),
        P("blk"),
    )
    return jax.shard_map(
        per_device,
        mesh=mesh,
        in_specs=placed,
        out_specs=(P("feat", "blk"), P("feat", "blk"), P("feat", None)),
        check_vma=False,
    )
```

```python
import functools
import math

import jax
import jax.numpy as jnp
from jax import lax
from jax.experimental import pallas as pl
from jax.experimental.pallas import tpu as pltpu
from jax.sharding import PartitionSpec as P

REACH = 4
GROUP = 8
WAVES = [[0, 2, -2], [1, 4, -4], [3, -1], [-3]]
MIB = 1 << 20


def stepped(block, forth):
    count = lax.axis_size("blk")
    route = [((i + (2 if forth == (i % 2 == 0) else -2)) % count, i) for i in range(count)]
    return lax.ppermute(block, "blk", route)


def flipped(block, axis, bit):
    return lax.ppermute(block, axis, [(i, i ^ bit) for i in range(lax.axis_size(axis))])


def exchanged_columns(array, place):
    q = array.shape[1] // 4
    b = [array[:, i * q : (i + 1) * q] for i in range(4)]
    swapped = jnp.concatenate([b[1], b[0], b[3], b[2]], axis=1)
    array = jnp.where(place % 2 == 1, swapped, array)
    halves = jnp.concatenate([array[:, 2 * q :], array[:, : 2 * q]], axis=1)
    return jnp.where(place // 2 == 1, halves, array)


COST = pl.CostEstimate(flops=0, transcendentals=0, bytes_accessed=6_000_000)
SMEM = pl.BlockSpec(memory_space=pltpu.SMEM)
VMEM = pl.BlockSpec(memory_space=pltpu.VMEM)


def near(array):
    return pltpu.with_memory_space_constraint(array, pltpu.VMEM)


def kept(mib):
    return pltpu.CompilerParams(vmem_limit_bytes=mib * MIB)


def plan_body(cap, row_ref, col_ref, off_ref, count_ref, sign_ref, list_ref, fill, home):
    sign = sign_ref[0]
    for w, wave in enumerate(WAVES):
        fill[w] = 0
        for j, offset in enumerate(wave):
            home[offset + REACH] = w + 16 * j

    def place(s, c):
        at_home = home[off_ref[s] * sign + REACH]
        wave = at_home & 15
        n = fill[wave]
        fill[wave] = n + 1
        list_ref[wave * cap + n] = (
            s + (row_ref[s] << 9) + (col_ref[s] << 15) + ((at_home >> 4) << 20)
        )
        return c

    lax.fori_loop(0, count_ref[0], place, 0)
    for w in range(len(WAVES)):
        n = fill[w]
        groups = (n + GROUP - 1) >> 3

        def pad(i, c):
            list_ref[w * cap + i] = 32 << 9
            return c

        lax.fori_loop(n, groups * GROUP, pad, 0)
        list_ref[len(WAVES) * cap + w] = groups


def plan(tile_row, tile_col, tile_off, tile_count, sign):
    cap = tile_row.shape[0] + GROUP
    return pl.pallas_call(
        functools.partial(plan_body, cap),
        out_shape=jax.ShapeDtypeStruct((len(WAVES) * cap + 16,), jnp.int32),
        in_specs=[SMEM] * 5,
        out_specs=SMEM,
        scratch_shapes=[pltpu.SMEM((16,), jnp.int32)] * 2,
        cost_estimate=COST,
        compiler_params=kept(2),
        name="plan",
    )(tile_row, tile_col, tile_off, tile_count, sign)


def tile_loop(wave, list_ref, vals_ref, multiply):
    cap = (list_ref.shape[0] - 16) // len(WAVES)

    def body(g, c):
        entries = [list_ref[wave * cap + g * GROUP + u] for u in range(GROUP)]
        multiply(entries, [vals_ref[e & 511] for e in entries])
        return c

    lax.fori_loop(0, list_ref[len(WAVES) * cap + wave], body, 0)


def column(tile):
    return pl.ds(pl.multiple_of(tile * 128, 128), 128)


def paired(first, second):
    zero = jnp.zeros_like(first)
    return jnp.concatenate(
        [jnp.concatenate([first, zero], axis=1), jnp.concatenate([zero, second], axis=1)], axis=0
    )


def forward_body(waves, parts, seeded, *refs):
    n = len(parts)
    list_ref, vals_ref = refs[:2]
    slabs, rest = refs[2 : 2 + sum(parts)], refs[2 + sum(parts) :]
    if seeded:
        seed_ref, rest = rest[0], rest[1:]
    out_ref, held = rest[:2]
    acc = rest[2] if len(rest) > 2 else out_ref
    acc[...] = seed_ref[...] if seeded else jnp.zeros_like(acc)
    at = 0
    for j, count in enumerate(parts):
        row = 0
        for slab in slabs[at : at + count]:
            held[j, row : row + slab.shape[0]] = slab[...]
            row += slab.shape[0]
        at += count
    feats = acc.shape[0]
    held[n, :, 0:128] = jnp.zeros((feats, 128), held.dtype)

    def multiply(first, entries, tiles):
        pieces = [
            held[jnp.where(((e >> 14) & 1) == 1, n, (e >> 20) + first), :, column((e >> 15) & 31)]
            for e in entries
        ]
        products = [
            lax.dot_general(
                paired(pieces[u], pieces[u + 1]),
                jnp.concatenate([tiles[u], tiles[u + 1]], axis=1),
                (((1,), (1,)), ((), ())),
                preferred_element_type=jnp.float32,
            )
            for u in range(0, GROUP, 2)
        ]
        for u, e in enumerate(entries):
            half = products[u // 2][u % 2 * feats : (u % 2 + 1) * feats]
            acc[:, column((e >> 9) & 31)] += half

    first = 0
    for wave in waves:
        tile_loop(wave, list_ref, vals_ref, functools.partial(multiply, first))
        first += len(WAVES[wave])
    if acc is not out_ref:
        out_ref[...] = acc[...].astype(out_ref.dtype)


def forward(waves, listed, vals, slabs, seed, dtype):
    feats, nodes = slabs[0][0].shape[0] * len(slabs[0]), slabs[0][0].shape[1]
    parts = [len(slab) for slab in slabs]
    flat = [part for slab in slabs for part in slab]
    return pl.pallas_call(
        functools.partial(forward_body, waves, parts, seed is not None),
        out_shape=pltpu.VMEM((feats, nodes), dtype),
        in_specs=[SMEM] + [VMEM] * (1 + len(flat) + (seed is not None)),
        out_specs=VMEM,
        scratch_shapes=[pltpu.VMEM((len(slabs) + 1, feats, nodes), flat[0].dtype)]
        + ([] if dtype == jnp.float32 else [pltpu.VMEM((feats, nodes), jnp.float32)]),
        cost_estimate=COST,
        compiler_params=kept(8),
        name=f"forward_{waves[0]}",
    )(listed, near(vals), *map(near, flat), *(() if seed is None else (near(seed),)))


def backward_body(wave, *refs):
    n = len(WAVES[wave])
    list_ref, vals_ref, grad_ref = refs[:3]
    outs, acc = refs[3:-1], refs[-1]
    acc[0:n] = jnp.zeros((n,) + acc.shape[1:], acc.dtype)
    feats = acc.shape[1]

    def multiply(entries, tiles):
        pieces = [grad_ref[:, column((e >> 9) & 31)] for e in entries]
        products = [
            jnp.dot(
                paired(pieces[u], pieces[u + 1]),
                jnp.concatenate([tiles[u], tiles[u + 1]], axis=0),
                preferred_element_type=jnp.float32,
            )
            for u in range(0, GROUP, 2)
        ]
        for u, e in enumerate(entries):
            half = products[u // 2][u % 2 * feats : (u % 2 + 1) * feats]
            acc[(e >> 20) + ((e >> 14) & 1) * n, :, column((e >> 15) & 31)] += half

    tile_loop(wave, list_ref, vals_ref, multiply)
    for j, out in enumerate(outs):
        out[...] = acc[j].astype(out.dtype)


def backward(wave, listed, vals, grad, dtypes):
    n = len(dtypes)
    return pl.pallas_call(
        functools.partial(backward_body, wave),
        out_shape=tuple(pltpu.VMEM(grad.shape, d) for d in dtypes),
        in_specs=[SMEM, VMEM, VMEM],
        out_specs=(VMEM,) * n,
        scratch_shapes=[pltpu.VMEM((n + 1,) + grad.shape, jnp.float32)],
        cost_estimate=COST,
        compiler_params=kept(8),
        name=f"backward_{wave}",
    )(listed, near(vals), near(grad))


def middle_body(factor, place_ref, *refs):
    ys, cots, weights, (out_ref, grad_ref, wgrad_ref) = refs[0:4], refs[4:8], refs[8:12], refs[12:]
    feats, nodes = ys[0].shape
    hidden = 4 * feats
    chunk = 512
    rows = [exchanged_columns(r[...], place_ref[0]) for r in weights]
    own_rows = rows[0]
    turned = jnp.concatenate(rows, axis=0).T
    wgrad = jnp.zeros((feats, hidden), jnp.float32)
    for start in range(0, nodes, chunk):
        here = slice(start, start + chunk)
        y = jnp.concatenate([r[:, here] for r in ys], axis=0)
        pre = jnp.dot(turned, y, preferred_element_type=jnp.float32)
        sig = jax.nn.sigmoid(pre)
        out_ref[:, here] = (pre[:feats] * sig[:feats]).astype(out_ref.dtype)
        cot = jnp.concatenate([r[:, here] for r in cots], axis=0).astype(jnp.float32)
        grad_pre = (cot * (sig * (1.0 + pre * (1.0 - sig)))).astype(jnp.bfloat16)
        grad_ref[:, here] = jnp.dot(
            own_rows, grad_pre, preferred_element_type=jnp.float32
        ).astype(grad_ref.dtype)
        wgrad += lax.dot_general(
            ys[0][:, here], grad_pre, (((1,), (1,)), ((), ())), preferred_element_type=jnp.float32
        )
    wgrad_ref[...] = exchanged_columns(wgrad, place_ref[0]) * factor


def middle(place, ys, cots, weights):
    feats, nodes = ys[0].shape
    factor = 1.0 / math.sqrt(nodes * lax.axis_size("blk"))
    return pl.pallas_call(
        functools.partial(middle_body, factor),
        out_shape=(
            jax.ShapeDtypeStruct((feats, nodes), jnp.bfloat16),
            pltpu.VMEM((feats, nodes), jnp.bfloat16),
            pltpu.VMEM((feats, 4 * feats), jnp.float32),
        ),
        in_specs=[SMEM] + [VMEM] * 12,
        out_specs=(VMEM,) * 3,
        cost_estimate=COST,
        compiler_params=kept(10),
        name="middle",
    )(place.astype(jnp.int32).reshape(1), *map(near, ys), *map(near, cots), *map(near, weights))


def fenced(*groups):
    return lax.optimization_barrier(groups)


def per_device(x_t, weight, cotangent, tile_row, tile_col, tile_off, tile_vals, tile_count):
    nodes = x_t.shape[1]
    f32, bf16 = jnp.float32, jnp.bfloat16
    place = lax.axis_index("feat")
    sign = (1 - 2 * (lax.axis_index("blk") % 2)).astype(jnp.int32).reshape(1)
    top, low = x_t[: x_t.shape[0] // 2], x_t[x_t.shape[0] // 2 :]
    u = [stepped(top, True), stepped(low, True)]
    x, v = flipped(x_t, "blk", 1), stepped(x_t, False)
    cot_far = flipped(cotangent, "feat", 2)
    listed = plan(tile_row, tile_col, tile_off, tile_count, sign)
    u[0], listed = fenced(u[0], listed)
    m = [stepped(half, True) for half in u]
    n = stepped(v, False)
    y = forward((0,), listed, tile_vals, [[x_t], u, [v]], None, f32)
    m[0], x, y, cot_far, weight = fenced(m[0], x, y, cot_far, weight)
    weight_far = flipped(weight, "feat", 2)
    mx = [flipped(half, "blk", 1) for half in m]
    xu, xv = stepped(x, True), stepped(x, False)
    y = forward((1,), listed, tile_vals, [[x], m, [n]], y, f32)
    weight, weight_far, y = fenced(weight, weight_far, y)
    cots = [cotangent, flipped(cotangent, "feat", 1), cot_far, flipped(cot_far, "feat", 1)]
    weights = [weight, flipped(weight, "feat", 1), weight_far, flipped(weight_far, "feat", 1)]
    y = forward((3,), listed, tile_vals, [mx], y, f32)
    y, cots, weights = fenced(y, cots, weights)
    y = forward((2,), listed, tile_vals, [[xu], [xv]], y, bf16)
    y_far = flipped(y, "feat", 2)
    ys = [y, flipped(y, "feat", 1), y_far, flipped(y_far, "feat", 1)]
    out_t, grad, wgrad = middle(place, ys, cots, weights)

    part = flipped(wgrad, "blk", 2)
    (to_mx,) = backward(3, listed, tile_vals, grad, [bf16])
    to_mx, grad = fenced(to_mx, grad)
    from_mx = flipped(to_mx, "blk", 1)
    to_xu, to_xv = backward(2, listed, tile_vals, grad, [bf16] * 2)
    to_xu, to_xv, grad, part = fenced(to_xu, to_xv, grad, part)
    from_xu, from_xv = stepped(to_xu, False), stepped(to_xv, True)
    wgrad = wgrad + part
    part = flipped(wgrad, "blk", 4)
    to_x, to_m, to_n = backward(1, listed, tile_vals, grad, [f32, f32, bf16])
    part, to_m, grad = fenced(part, to_m, grad)
    wgrad = wgrad + part
    part = flipped(wgrad, "blk", 8)
    total, to_u, to_v = backward(0, listed, tile_vals, grad, [f32] * 3)
    from_mx, from_xu, from_xv, to_m, to_n, total, to_x, to_u, to_v, part = fenced(
        from_mx, from_xu, from_xv, to_m, to_n, total, to_x, to_u, to_v, part
    )
    from_m = stepped((to_m + from_mx.astype(f32)).astype(bf16), False)
    from_n = stepped(to_n, True)
    to_x = (to_x + from_xu.astype(f32) + from_xv.astype(f32)).astype(bf16)
    wgrad = wgrad + part
    wgrad = wgrad + flipped(wgrad, "blk", 1)
    wgrad = wgrad + flipped(wgrad, "blk", 16)
    from_m, from_n, to_x, to_u, to_v, wgrad = fenced(from_m, from_n, to_x, to_u, to_v, wgrad)
    part = flipped(wgrad, "blk", 32)
    from_u = stepped((to_u + from_m.astype(f32)).astype(bf16), False)
    from_v = stepped((to_v + from_n.astype(f32)).astype(bf16), True)
    from_x = flipped(to_x, "blk", 1)
    wgrad = wgrad + part
    total = total + from_u.astype(f32) + from_v.astype(f32) + from_x.astype(f32)
    return (out_t, total.astype(bf16), wgrad)


def solution(mesh):
    placed = (
        P("feat", "blk"),
        P("feat", None),
        P("feat", "blk"),
        P("blk"),
        P("blk"),
        P("blk"),
        P("blk", None, None),
        P("blk"),
    )
    return jax.shard_map(
        per_device,
        mesh=mesh,
        in_specs=placed,
        out_specs=(P("feat", "blk"), P("feat", "blk"), P("feat", None)),
        check_vma=False,
    )
```

```python
import functools
import math

import jax
import jax.numpy as jnp
from jax import lax
from jax.experimental import pallas as pl
from jax.experimental.pallas import tpu as pltpu
from jax.sharding import PartitionSpec as P

REACH = 4
GROUP = 8
WAVES = [[0, 1, 2, -2], [4, -4], [3, -1, -3]]
MIB = 1 << 20


def stepped(block, forth):
    count = lax.axis_size("blk")
    route = [((i + (2 if forth == (i % 2 == 0) else -2)) % count, i) for i in range(count)]
    return lax.ppermute(block, "blk", route)


def flipped(block, axis, bit):
    return lax.ppermute(block, axis, [(i, i ^ bit) for i in range(lax.axis_size(axis))])


def exchanged_columns(array, place):
    q = array.shape[1] // 4
    b = [array[:, i * q : (i + 1) * q] for i in range(4)]
    swapped = jnp.concatenate([b[1], b[0], b[3], b[2]], axis=1)
    array = jnp.where(place % 2 == 1, swapped, array)
    halves = jnp.concatenate([array[:, 2 * q :], array[:, : 2 * q]], axis=1)
    return jnp.where(place // 2 == 1, halves, array)


COST = pl.CostEstimate(flops=0, transcendentals=0, bytes_accessed=6_000_000)
SMEM = pl.BlockSpec(memory_space=pltpu.SMEM)
VMEM = pl.BlockSpec(memory_space=pltpu.VMEM)


def near(array):
    return pltpu.with_memory_space_constraint(array, pltpu.VMEM)


def kept(mib):
    return pltpu.CompilerParams(vmem_limit_bytes=mib * MIB)


def plan_body(cap, row_ref, col_ref, off_ref, count_ref, sign_ref, list_ref, fill, home):
    sign = sign_ref[0]
    for w, wave in enumerate(WAVES):
        fill[w] = 0
        for j, offset in enumerate(wave):
            home[offset + REACH] = w + 16 * j

    def place(s, c):
        at_home = home[off_ref[s] * sign + REACH]
        wave = at_home & 15
        n = fill[wave]
        fill[wave] = n + 1
        list_ref[wave * cap + n] = (
            s + (row_ref[s] << 9) + (col_ref[s] << 15) + ((at_home >> 4) << 20)
        )
        return c

    lax.fori_loop(0, count_ref[0], place, 0)
    for w in range(len(WAVES)):
        n = fill[w]
        groups = (n + GROUP - 1) >> 3

        def pad(i, c):
            list_ref[w * cap + i] = 32 << 9
            return c

        lax.fori_loop(n, groups * GROUP, pad, 0)
        list_ref[len(WAVES) * cap + w] = groups


def plan(tile_row, tile_col, tile_off, tile_count, sign):
    cap = tile_row.shape[0] + GROUP
    return pl.pallas_call(
        functools.partial(plan_body, cap),
        out_shape=jax.ShapeDtypeStruct((len(WAVES) * cap + 16,), jnp.int32),
        in_specs=[SMEM] * 5,
        out_specs=SMEM,
        scratch_shapes=[pltpu.SMEM((16,), jnp.int32)] * 2,
        cost_estimate=COST,
        compiler_params=kept(2),
        name="plan",
    )(tile_row, tile_col, tile_off, tile_count, sign)


def tile_loop(wave, list_ref, vals_ref, multiply):
    cap = (list_ref.shape[0] - 16) // len(WAVES)

    def body(g, c):
        entries = [list_ref[wave * cap + g * GROUP + u] for u in range(GROUP)]
        multiply(entries, [vals_ref[e & 511] for e in entries])
        return c

    lax.fori_loop(0, list_ref[len(WAVES) * cap + wave], body, 0)


def column(tile):
    return pl.ds(pl.multiple_of(tile * 128, 128), 128)


def paired(first, second):
    zero = jnp.zeros_like(first)
    return jnp.concatenate(
        [jnp.concatenate([first, zero], axis=1), jnp.concatenate([zero, second], axis=1)], axis=0
    )


def forward_body(wave, seeded, *refs):
    n = len(WAVES[wave])
    list_ref, vals_ref = refs[:2]
    slabs, rest = refs[2 : 2 + n], refs[2 + n :]
    if seeded:
        seed_ref, rest = rest[0], rest[1:]
    out_ref, held = rest[:2]
    acc = rest[2] if len(rest) > 2 else out_ref
    acc[...] = seed_ref[...] if seeded else jnp.zeros_like(acc)
    for j, slab in enumerate(slabs):
        held[j] = slab[...]
    feats = acc.shape[0]
    held[n, :, 0:128] = jnp.zeros((feats, 128), held.dtype)

    def multiply(entries, tiles):
        pieces = [
            held[(e >> 20) + ((e >> 14) & 1) * n, :, column((e >> 15) & 31)] for e in entries
        ]
        products = [
            lax.dot_general(
                paired(pieces[u], pieces[u + 1]),
                jnp.concatenate([tiles[u], tiles[u + 1]], axis=1),
                (((1,), (1,)), ((), ())),
                preferred_element_type=jnp.float32,
            )
            for u in range(0, GROUP, 2)
        ]
        for u, e in enumerate(entries):
            half = products[u // 2][u % 2 * feats : (u % 2 + 1) * feats]
            acc[:, column((e >> 9) & 31)] += half

    tile_loop(wave, list_ref, vals_ref, multiply)
    if acc is not out_ref:
        out_ref[...] = acc[...].astype(out_ref.dtype)


def forward(wave, listed, vals, slabs, seed, dtype):
    feats, nodes = slabs[0].shape
    wide = dtype == jnp.float32
    return pl.pallas_call(
        functools.partial(forward_body, wave, seed is not None),
        out_shape=pltpu.VMEM((feats, nodes), dtype),
        in_specs=[SMEM] + [VMEM] * (1 + len(slabs) + (seed is not None)),
        out_specs=VMEM,
        scratch_shapes=[pltpu.VMEM((len(slabs) + 1, feats, nodes), slabs[0].dtype)]
        + ([] if wide else [pltpu.VMEM((feats, nodes), jnp.float32)]),
        cost_estimate=COST,
        compiler_params=kept(8),
        name=f"forward_{wave}",
    )(listed, near(vals), *map(near, slabs), *(() if seed is None else (near(seed),)))


def backward_body(wave, *refs):
    n = len(WAVES[wave])
    list_ref, vals_ref, grad_ref = refs[:3]
    outs, acc = refs[3:-1], refs[-1]
    acc[0:n] = jnp.zeros((n,) + acc.shape[1:], acc.dtype)
    feats = acc.shape[1]

    def multiply(entries, tiles):
        pieces = [grad_ref[:, column((e >> 9) & 31)] for e in entries]
        products = [
            jnp.dot(
                paired(pieces[u], pieces[u + 1]),
                jnp.concatenate([tiles[u], tiles[u + 1]], axis=0),
                preferred_element_type=jnp.float32,
            )
            for u in range(0, GROUP, 2)
        ]
        for u, e in enumerate(entries):
            half = products[u // 2][u % 2 * feats : (u % 2 + 1) * feats]
            acc[(e >> 20) + ((e >> 14) & 1) * n, :, column((e >> 15) & 31)] += half

    tile_loop(wave, list_ref, vals_ref, multiply)
    for j, out in enumerate(outs):
        out[...] = acc[j].astype(out.dtype)


def backward(wave, listed, vals, grad, dtypes):
    n = len(dtypes)
    return pl.pallas_call(
        functools.partial(backward_body, wave),
        out_shape=tuple(pltpu.VMEM(grad.shape, d) for d in dtypes),
        in_specs=[SMEM, VMEM, VMEM],
        out_specs=(VMEM,) * n,
        scratch_shapes=[pltpu.VMEM((n + 1,) + grad.shape, jnp.float32)],
        cost_estimate=COST,
        compiler_params=kept(8),
        name=f"backward_{wave}",
    )(listed, near(vals), near(grad))


def middle_body(factor, place_ref, *refs):
    ys, packed, (out_ref, grad_ref, wgrad_ref) = refs[0:4], refs[4:8], refs[8:]
    feats, nodes = ys[0].shape
    hidden = 4 * feats
    chunk = 512
    rows = []
    for k in range(4):
        w = packed[k][:, nodes:]
        rows.append(
            jnp.concatenate(
                [w[:, (j ^ k) * feats : ((j ^ k) + 1) * feats] for j in range(4)], axis=1
            )
        )
    own_rows = rows[0]
    turned = jnp.concatenate(rows, axis=0).T
    wgrad = jnp.zeros((feats, hidden), jnp.float32)
    for start in range(0, nodes, chunk):
        here = slice(start, start + chunk)
        y = jnp.concatenate([r[:, here] for r in ys], axis=0)
        pre = jnp.dot(turned, y, preferred_element_type=jnp.float32)
        sig = jax.nn.sigmoid(pre)
        out_ref[:, here] = (pre[:feats] * sig[:feats]).astype(out_ref.dtype)
        cot = jnp.concatenate([r[:, here] for r in packed], axis=0).astype(jnp.float32)
        grad_pre = (cot * (sig * (1.0 + pre * (1.0 - sig)))).astype(jnp.bfloat16)
        grad_ref[:, here] = jnp.dot(
            own_rows, grad_pre, preferred_element_type=jnp.float32
        ).astype(grad_ref.dtype)
        wgrad += lax.dot_general(
            ys[0][:, here], grad_pre, (((1,), (1,)), ((), ())), preferred_element_type=jnp.float32
        )
    wgrad_ref[...] = exchanged_columns(wgrad, place_ref[0]) * factor


def middle(place, ys, packed):
    feats, nodes = ys[0].shape
    factor = 1.0 / math.sqrt(nodes * lax.axis_size("blk"))
    return pl.pallas_call(
        functools.partial(middle_body, factor),
        out_shape=(
            jax.ShapeDtypeStruct((feats, nodes), jnp.bfloat16),
            pltpu.VMEM((feats, nodes), jnp.bfloat16),
            pltpu.VMEM((feats, 4 * feats), jnp.float32),
        ),
        in_specs=[SMEM] + [VMEM] * 8,
        out_specs=(VMEM,) * 3,
        cost_estimate=COST,
        compiler_params=kept(10),
        name="middle",
    )(place.astype(jnp.int32).reshape(1), *map(near, ys), *map(near, packed))


def fenced(*groups):
    return lax.optimization_barrier(groups)


def per_device(x_t, weight, cotangent, tile_row, tile_col, tile_off, tile_vals, tile_count):
    nodes = x_t.shape[1]
    f32, bf16 = jnp.float32, jnp.bfloat16
    place = lax.axis_index("feat")
    sign = (1 - 2 * (lax.axis_index("blk") % 2)).astype(jnp.int32).reshape(1)
    own = jnp.concatenate([cotangent, exchanged_columns(weight, place)], axis=1)

    x, u, v = flipped(x_t, "blk", 1), stepped(x_t, True), stepped(x_t, False)
    listed = plan(tile_row, tile_col, tile_off, tile_count, sign)
    x, u, v, listed, own = fenced(x, u, v, listed, own)
    m, n, far = stepped(u, True), stepped(v, False), flipped(own, "feat", 2)
    y = forward(0, listed, tile_vals, [x_t, x, u, v], None, f32)
    m, n, y, x, far, own = fenced(m, n, y, x, far, own)
    mx, xu, xv = flipped(m, "blk", 1), stepped(x, True), stepped(x, False)
    y = forward(1, listed, tile_vals, [m, n], y, f32)
    packed = [own, flipped(own, "feat", 1), far, flipped(far, "feat", 1)]
    xu, xv, mx, y, packed = fenced(xu, xv, mx, y, packed)
    y = forward(2, listed, tile_vals, [xu, xv, mx], y, bf16)
    y_far = flipped(y, "feat", 2)
    ys = [y, flipped(y, "feat", 1), y_far, flipped(y_far, "feat", 1)]
    out_t, grad, wgrad = middle(place, ys, packed)

    part = flipped(wgrad, "blk", 2)
    to_xu, to_xv, to_mx = backward(2, listed, tile_vals, grad, [bf16] * 3)
    to_xu, to_xv, to_mx, part, grad = fenced(to_xu, to_xv, to_mx, part, grad)
    from_mx, from_xu, from_xv = flipped(to_mx, "blk", 1), stepped(to_xu, False), stepped(to_xv, True)
    wgrad = wgrad + part
    part = flipped(wgrad, "blk", 8)
    to_m, to_n = backward(1, listed, tile_vals, grad, [f32, bf16])
    part, to_m, grad = fenced(part, to_m, grad)
    wgrad = wgrad + part
    part = flipped(wgrad, "blk", 16)
    total, to_x, to_u, to_v = backward(0, listed, tile_vals, grad, [f32] * 4)
    from_mx, from_xu, from_xv, to_m, to_n, total, to_x, to_u, to_v, part = fenced(
        from_mx, from_xu, from_xv, to_m, to_n, total, to_x, to_u, to_v, part
    )
    from_m = stepped((to_m + from_mx.astype(f32)).astype(bf16), False)
    from_n = stepped(to_n, True)
    to_x = (to_x + from_xu.astype(f32) + from_xv.astype(f32)).astype(bf16)
    wgrad = wgrad + part
    wgrad = wgrad + flipped(wgrad, "blk", 1)
    wgrad = wgrad + flipped(wgrad, "blk", 4)
    from_m, from_n, to_x, to_u, to_v, wgrad = fenced(from_m, from_n, to_x, to_u, to_v, wgrad)
    part = flipped(wgrad, "blk", 32)
    from_u = stepped((to_u + from_m.astype(f32)).astype(bf16), False)
    from_v = stepped((to_v + from_n.astype(f32)).astype(bf16), True)
    from_x = flipped(to_x, "blk", 1)
    wgrad = wgrad + part
    total = total + from_u.astype(f32) + from_v.astype(f32) + from_x.astype(f32)
    return (out_t, total.astype(bf16), wgrad)


def solution(mesh):
    placed = (
        P("feat", "blk"),
        P("feat", None),
        P("feat", "blk"),
        P("blk"),
        P("blk"),
        P("blk"),
        P("blk", None, None),
        P("blk"),
    )
    return jax.shard_map(
        per_device,
        mesh=mesh,
        in_specs=placed,
        out_specs=(P("feat", "blk"), P("feat", "blk"), P("feat", None)),
        check_vma=False,
    )
```

```python
import functools
import math

import jax
import jax.numpy as jnp
from jax import lax
from jax.experimental import pallas as pl
from jax.experimental.pallas import tpu as pltpu
from jax.sharding import PartitionSpec as P

REACH = 4
GROUP = 8
WAVES = [[0, 2, -2], [1, 4, -4], [3, -1, -3]]
MIB = 1 << 20


def stepped(block, forth):
    count = lax.axis_size("blk")
    route = [((i + (2 if forth == (i % 2 == 0) else -2)) % count, i) for i in range(count)]
    return lax.ppermute(block, "blk", route)


def flipped(block, axis, bit):
    return lax.ppermute(block, axis, [(i, i ^ bit) for i in range(lax.axis_size(axis))])


def exchanged_columns(array, place):
    q = array.shape[1] // 4
    b = [array[:, i * q : (i + 1) * q] for i in range(4)]
    swapped = jnp.concatenate([b[1], b[0], b[3], b[2]], axis=1)
    array = jnp.where(place % 2 == 1, swapped, array)
    halves = jnp.concatenate([array[:, 2 * q :], array[:, : 2 * q]], axis=1)
    return jnp.where(place // 2 == 1, halves, array)


COST = pl.CostEstimate(flops=0, transcendentals=0, bytes_accessed=6_000_000)
SMEM = pl.BlockSpec(memory_space=pltpu.SMEM)
VMEM = pl.BlockSpec(memory_space=pltpu.VMEM)


def near(array):
    return pltpu.with_memory_space_constraint(array, pltpu.VMEM)


def kept(mib):
    return pltpu.CompilerParams(vmem_limit_bytes=mib * MIB)


def plan_body(cap, row_ref, col_ref, off_ref, count_ref, sign_ref, list_ref, fill, home):
    sign = sign_ref[0]
    for w, wave in enumerate(WAVES):
        fill[w] = 0
        for j, offset in enumerate(wave):
            home[offset + REACH] = w + 16 * j

    def place(s, c):
        at_home = home[off_ref[s] * sign + REACH]
        wave = at_home & 15
        n = fill[wave]
        fill[wave] = n + 1
        list_ref[wave * cap + n] = (
            s + (row_ref[s] << 9) + (col_ref[s] << 15) + ((at_home >> 4) << 20)
        )
        return c

    lax.fori_loop(0, count_ref[0], place, 0)
    for w in range(len(WAVES)):
        n = fill[w]
        groups = (n + GROUP - 1) >> 3

        def pad(i, c):
            list_ref[w * cap + i] = 32 << 9
            return c

        lax.fori_loop(n, groups * GROUP, pad, 0)
        list_ref[len(WAVES) * cap + w] = groups


def plan(tile_row, tile_col, tile_off, tile_count, sign):
    cap = tile_row.shape[0] + GROUP
    return pl.pallas_call(
        functools.partial(plan_body, cap),
        out_shape=jax.ShapeDtypeStruct((len(WAVES) * cap + 16,), jnp.int32),
        in_specs=[SMEM] * 5,
        out_specs=SMEM,
        scratch_shapes=[pltpu.SMEM((16,), jnp.int32)] * 2,
        cost_estimate=COST,
        compiler_params=kept(2),
        name="plan",
    )(tile_row, tile_col, tile_off, tile_count, sign)


def tile_loop(wave, list_ref, vals_ref, multiply):
    cap = (list_ref.shape[0] - 16) // len(WAVES)

    def body(g, c):
        entries = [list_ref[wave * cap + g * GROUP + u] for u in range(GROUP)]
        multiply(entries, [vals_ref[e & 511] for e in entries])
        return c

    lax.fori_loop(0, list_ref[len(WAVES) * cap + wave], body, 0)


def column(tile):
    return pl.ds(pl.multiple_of(tile * 128, 128), 128)


def paired(first, second):
    zero = jnp.zeros_like(first)
    return jnp.concatenate(
        [jnp.concatenate([first, zero], axis=1), jnp.concatenate([zero, second], axis=1)], axis=0
    )


def forward_body(wave, seeded, *refs):
    n = len(WAVES[wave])
    list_ref, vals_ref = refs[:2]
    slabs, rest = refs[2 : 2 + n], refs[2 + n :]
    if seeded:
        seed_ref, rest = rest[0], rest[1:]
    out_ref, held = rest[:2]
    acc = rest[2] if len(rest) > 2 else out_ref
    acc[...] = seed_ref[...] if seeded else jnp.zeros_like(acc)
    for j, slab in enumerate(slabs):
        held[j] = slab[...]
    feats = acc.shape[0]
    held[n, :, 0:128] = jnp.zeros((feats, 128), held.dtype)

    def multiply(entries, tiles):
        pieces = [
            held[(e >> 20) + ((e >> 14) & 1) * n, :, column((e >> 15) & 31)] for e in entries
        ]
        products = [
            lax.dot_general(
                paired(pieces[u], pieces[u + 1]),
                jnp.concatenate([tiles[u], tiles[u + 1]], axis=1),
                (((1,), (1,)), ((), ())),
                preferred_element_type=jnp.float32,
            )
            for u in range(0, GROUP, 2)
        ]
        for u, e in enumerate(entries):
            half = products[u // 2][u % 2 * feats : (u % 2 + 1) * feats]
            acc[:, column((e >> 9) & 31)] += half

    tile_loop(wave, list_ref, vals_ref, multiply)
    if acc is not out_ref:
        out_ref[...] = acc[...].astype(out_ref.dtype)


def forward(wave, listed, vals, slabs, seed, dtype):
    feats, nodes = slabs[0].shape
    wide = dtype == jnp.float32
    return pl.pallas_call(
        functools.partial(forward_body, wave, seed is not None),
        out_shape=pltpu.VMEM((feats, nodes), dtype),
        in_specs=[SMEM] + [VMEM] * (1 + len(slabs) + (seed is not None)),
        out_specs=VMEM,
        scratch_shapes=[pltpu.VMEM((len(slabs) + 1, feats, nodes), slabs[0].dtype)]
        + ([] if wide else [pltpu.VMEM((feats, nodes), jnp.float32)]),
        cost_estimate=COST,
        compiler_params=kept(8),
        name=f"forward_{wave}",
    )(listed, near(vals), *map(near, slabs), *(() if seed is None else (near(seed),)))


def backward_body(wave, *refs):
    n = len(WAVES[wave])
    list_ref, vals_ref, grad_ref = refs[:3]
    outs, acc = refs[3:-1], refs[-1]
    acc[0:n] = jnp.zeros((n,) + acc.shape[1:], acc.dtype)
    feats = acc.shape[1]

    def multiply(entries, tiles):
        pieces = [grad_ref[:, column((e >> 9) & 31)] for e in entries]
        products = [
            jnp.dot(
                paired(pieces[u], pieces[u + 1]),
                jnp.concatenate([tiles[u], tiles[u + 1]], axis=0),
                preferred_element_type=jnp.float32,
            )
            for u in range(0, GROUP, 2)
        ]
        for u, e in enumerate(entries):
            half = products[u // 2][u % 2 * feats : (u % 2 + 1) * feats]
            acc[(e >> 20) + ((e >> 14) & 1) * n, :, column((e >> 15) & 31)] += half

    tile_loop(wave, list_ref, vals_ref, multiply)
    for j, out in enumerate(outs):
        out[...] = acc[j].astype(out.dtype)


def backward(wave, listed, vals, grad, dtypes):
    n = len(dtypes)
    return pl.pallas_call(
        functools.partial(backward_body, wave),
        out_shape=tuple(pltpu.VMEM(grad.shape, d) for d in dtypes),
        in_specs=[SMEM, VMEM, VMEM],
        out_specs=(VMEM,) * n,
        scratch_shapes=[pltpu.VMEM((n + 1,) + grad.shape, jnp.float32)],
        cost_estimate=COST,
        compiler_params=kept(8),
        name=f"backward_{wave}",
    )(listed, near(vals), near(grad))


def middle_body(factor, place_ref, *refs):
    ys, packed, (out_ref, grad_ref, wgrad_ref) = refs[0:4], refs[4:8], refs[8:]
    feats, nodes = ys[0].shape
    hidden = 4 * feats
    chunk = 512
    rows = []
    for k in range(4):
        w = packed[k][:, nodes:]
        rows.append(
            jnp.concatenate(
                [w[:, (j ^ k) * feats : ((j ^ k) + 1) * feats] for j in range(4)], axis=1
            )
        )
    own_rows = rows[0]
    turned = jnp.concatenate(rows, axis=0).T
    wgrad = jnp.zeros((feats, hidden), jnp.float32)
    for start in range(0, nodes, chunk):
        here = slice(start, start + chunk)
        y = jnp.concatenate([r[:, here] for r in ys], axis=0)
        pre = jnp.dot(turned, y, preferred_element_type=jnp.float32)
        sig = jax.nn.sigmoid(pre)
        out_ref[:, here] = (pre[:feats] * sig[:feats]).astype(out_ref.dtype)
        cot = jnp.concatenate([r[:, here] for r in packed], axis=0).astype(jnp.float32)
        grad_pre = (cot * (sig * (1.0 + pre * (1.0 - sig)))).astype(jnp.bfloat16)
        grad_ref[:, here] = jnp.dot(
            own_rows, grad_pre, preferred_element_type=jnp.float32
        ).astype(grad_ref.dtype)
        wgrad += lax.dot_general(
            ys[0][:, here], grad_pre, (((1,), (1,)), ((), ())), preferred_element_type=jnp.float32
        )
    wgrad_ref[...] = exchanged_columns(wgrad, place_ref[0]) * factor


def middle(place, ys, packed):
    feats, nodes = ys[0].shape
    factor = 1.0 / math.sqrt(nodes * lax.axis_size("blk"))
    return pl.pallas_call(
        functools.partial(middle_body, factor),
        out_shape=(
            jax.ShapeDtypeStruct((feats, nodes), jnp.bfloat16),
            pltpu.VMEM((feats, nodes), jnp.bfloat16),
            pltpu.VMEM((feats, 4 * feats), jnp.float32),
        ),
        in_specs=[SMEM] + [VMEM] * 8,
        out_specs=(VMEM,) * 3,
        cost_estimate=COST,
        compiler_params=kept(10),
        name="middle",
    )(place.astype(jnp.int32).reshape(1), *map(near, ys), *map(near, packed))


def fenced(*groups):
    return lax.optimization_barrier(groups)


def per_device(x_t, weight, cotangent, tile_row, tile_col, tile_off, tile_vals, tile_count):
    nodes = x_t.shape[1]
    f32, bf16 = jnp.float32, jnp.bfloat16
    place = lax.axis_index("feat")
    sign = (1 - 2 * (lax.axis_index("blk") % 2)).astype(jnp.int32).reshape(1)
    own = jnp.concatenate([cotangent, exchanged_columns(weight, place)], axis=1)

    x, u, v = flipped(x_t, "blk", 1), stepped(x_t, True), stepped(x_t, False)
    far = flipped(own, "feat", 2)
    listed = plan(tile_row, tile_col, tile_off, tile_count, sign)
    u, v, listed = fenced(u, v, listed)
    m, n = stepped(u, True), stepped(v, False)
    y = forward(0, listed, tile_vals, [x_t, u, v], None, f32)
    m, n, y, x, far, own = fenced(m, n, y, x, far, own)
    mx, xu, xv = flipped(m, "blk", 1), stepped(x, True), stepped(x, False)
    y = forward(1, listed, tile_vals, [x, m, n], y, f32)
    packed = [own, flipped(own, "feat", 1), far, flipped(far, "feat", 1)]
    xu, xv, mx, y, packed = fenced(xu, xv, mx, y, packed)
    y = forward(2, listed, tile_vals, [xu, xv, mx], y, bf16)
    y_far = flipped(y, "feat", 2)
    ys = [y, flipped(y, "feat", 1), y_far, flipped(y_far, "feat", 1)]
    out_t, grad, wgrad = middle(place, ys, packed)

    parts = [flipped(wgrad, "blk", bit) for bit in (2, 4, 6)]
    to_xu, to_xv, to_mx = backward(2, listed, tile_vals, grad, [bf16] * 3)
    to_xu, to_xv, to_mx, parts, grad = fenced(to_xu, to_xv, to_mx, parts, grad)
    from_mx, from_xu, from_xv = flipped(to_mx, "blk", 1), stepped(to_xu, False), stepped(to_xv, True)
    wgrad = (wgrad + parts[0]) + (parts[1] + parts[2])
    part = flipped(wgrad, "blk", 8)
    to_x, to_m, to_n = backward(1, listed, tile_vals, grad, [f32, f32, bf16])
    from_mx, from_xu, from_xv, to_m, to_n, to_x, grad, part = fenced(
        from_mx, from_xu, from_xv, to_m, to_n, to_x, grad, part
    )
    from_m = stepped((to_m + from_mx.astype(f32)).astype(bf16), False)
    from_n = stepped(to_n, True)
    total, to_u, to_v = backward(0, listed, tile_vals, grad, [f32] * 3)
    from_x = flipped((to_x + from_xu.astype(f32) + from_xv.astype(f32)).astype(bf16), "blk", 1)
    wgrad = wgrad + part
    part = flipped(wgrad, "blk", 16)
    total, to_u, to_v, part = fenced(total, to_u, to_v, part)
    wgrad = wgrad + part
    part = flipped(wgrad, "blk", 32)
    from_m, from_n, to_u, to_v, part = fenced(from_m, from_n, to_u, to_v, part)
    wgrad = wgrad + part
    part = flipped(wgrad, "blk", 1)
    from_u = stepped((to_u + from_m.astype(f32)).astype(bf16), False)
    from_v = stepped((to_v + from_n.astype(f32)).astype(bf16), True)
    wgrad = wgrad + part
    total = total + from_u.astype(f32) + from_v.astype(f32) + from_x.astype(f32)
    return (out_t, total.astype(bf16), wgrad)


def solution(mesh):
    placed = (
        P("feat", "blk"),
        P("feat", None),
        P("feat", "blk"),
        P("blk"),
        P("blk"),
        P("blk"),
        P("blk", None, None),
        P("blk"),
    )
    return jax.shard_map(
        per_device,
        mesh=mesh,
        in_specs=placed,
        out_specs=(P("feat", "blk"), P("feat", "blk"), P("feat", None)),
        check_vma=False,
    )
```

```python
import functools
import math

import jax
import jax.numpy as jnp
from jax import lax
from jax.experimental import pallas as pl
from jax.experimental.pallas import tpu as pltpu
from jax.sharding import PartitionSpec as P

REACH = 4
GROUP = 8
WAVES = [[0, 2, -2], [1, 4, -4], [3, -1, -3]]
MIB = 1 << 20


def stepped(block, forth):
    count = lax.axis_size("blk")
    route = [((i + (2 if forth == (i % 2 == 0) else -2)) % count, i) for i in range(count)]
    return lax.ppermute(block, "blk", route)


def flipped(block, axis, bit):
    return lax.ppermute(block, axis, [(i, i ^ bit) for i in range(lax.axis_size(axis))])


def exchanged_columns(array, place):
    q = array.shape[1] // 4
    b = [array[:, i * q : (i + 1) * q] for i in range(4)]
    swapped = jnp.concatenate([b[1], b[0], b[3], b[2]], axis=1)
    array = jnp.where(place % 2 == 1, swapped, array)
    halves = jnp.concatenate([array[:, 2 * q :], array[:, : 2 * q]], axis=1)
    return jnp.where(place // 2 == 1, halves, array)


COST = pl.CostEstimate(flops=0, transcendentals=0, bytes_accessed=6_000_000)
SMEM = pl.BlockSpec(memory_space=pltpu.SMEM)
VMEM = pl.BlockSpec(memory_space=pltpu.VMEM)


def near(array):
    return pltpu.with_memory_space_constraint(array, pltpu.VMEM)


def kept(mib):
    return pltpu.CompilerParams(vmem_limit_bytes=mib * MIB)


def plan_body(cap, row_ref, col_ref, off_ref, count_ref, sign_ref, list_ref, fill, home):
    sign = sign_ref[0]
    for w, wave in enumerate(WAVES):
        fill[w] = 0
        for j, offset in enumerate(wave):
            home[offset + REACH] = w + 16 * j

    def place(s, c):
        at_home = home[off_ref[s] * sign + REACH]
        wave = at_home & 15
        n = fill[wave]
        fill[wave] = n + 1
        list_ref[wave * cap + n] = (
            s + (row_ref[s] << 9) + (col_ref[s] << 15) + ((at_home >> 4) << 20)
        )
        return c

    lax.fori_loop(0, count_ref[0], place, 0)
    for w in range(len(WAVES)):
        n = fill[w]
        groups = (n + GROUP - 1) >> 3

        def pad(i, c):
            list_ref[w * cap + i] = 32 << 9
            return c

        lax.fori_loop(n, groups * GROUP, pad, 0)
        list_ref[len(WAVES) * cap + w] = groups


def plan(tile_row, tile_col, tile_off, tile_count, sign):
    cap = tile_row.shape[0] + GROUP
    return pl.pallas_call(
        functools.partial(plan_body, cap),
        out_shape=jax.ShapeDtypeStruct((len(WAVES) * cap + 16,), jnp.int32),
        in_specs=[SMEM] * 5,
        out_specs=SMEM,
        scratch_shapes=[pltpu.SMEM((16,), jnp.int32)] * 2,
        cost_estimate=COST,
        compiler_params=kept(2),
        name="plan",
    )(tile_row, tile_col, tile_off, tile_count, sign)


def tile_loop(wave, list_ref, vals_ref, multiply):
    cap = (list_ref.shape[0] - 16) // len(WAVES)

    def body(g, c):
        entries = [list_ref[wave * cap + g * GROUP + u] for u in range(GROUP)]
        multiply(entries, [vals_ref[e & 511] for e in entries])
        return c

    lax.fori_loop(0, list_ref[len(WAVES) * cap + wave], body, 0)


def column(tile):
    return pl.ds(pl.multiple_of(tile * 128, 128), 128)


def paired(first, second):
    zero = jnp.zeros_like(first)
    return jnp.concatenate(
        [jnp.concatenate([first, zero], axis=1), jnp.concatenate([zero, second], axis=1)], axis=0
    )


def forward_body(wave, seeded, *refs):
    n = len(WAVES[wave])
    list_ref, vals_ref = refs[:2]
    slabs, rest = refs[2 : 2 + n], refs[2 + n :]
    if seeded:
        seed_ref, rest = rest[0], rest[1:]
    out_ref, held = rest[:2]
    acc = rest[2] if len(rest) > 2 else out_ref
    acc[...] = seed_ref[...] if seeded else jnp.zeros_like(acc)
    for j, slab in enumerate(slabs):
        held[j] = slab[...]
    feats = acc.shape[0]
    held[n, :, 0:128] = jnp.zeros((feats, 128), held.dtype)

    def multiply(entries, tiles):
        pieces = [
            held[(e >> 20) + ((e >> 14) & 1) * n, :, column((e >> 15) & 31)] for e in entries
        ]
        products = [
            lax.dot_general(
                paired(pieces[u], pieces[u + 1]),
                jnp.concatenate([tiles[u], tiles[u + 1]], axis=1),
                (((1,), (1,)), ((), ())),
                preferred_element_type=jnp.float32,
            )
            for u in range(0, GROUP, 2)
        ]
        for u, e in enumerate(entries):
            half = products[u // 2][u % 2 * feats : (u % 2 + 1) * feats]
            acc[:, column((e >> 9) & 31)] += half

    tile_loop(wave, list_ref, vals_ref, multiply)
    if acc is not out_ref:
        out_ref[...] = acc[...].astype(out_ref.dtype)


def forward(wave, listed, vals, slabs, seed, dtype):
    feats, nodes = slabs[0].shape
    wide = dtype == jnp.float32
    return pl.pallas_call(
        functools.partial(forward_body, wave, seed is not None),
        out_shape=pltpu.VMEM((feats, nodes), dtype),
        in_specs=[SMEM] + [VMEM] * (1 + len(slabs) + (seed is not None)),
        out_specs=VMEM,
        scratch_shapes=[pltpu.VMEM((len(slabs) + 1, feats, nodes), slabs[0].dtype)]
        + ([] if wide else [pltpu.VMEM((feats, nodes), jnp.float32)]),
        cost_estimate=COST,
        compiler_params=kept(8),
        name=f"forward_{wave}",
    )(listed, near(vals), *map(near, slabs), *(() if seed is None else (near(seed),)))


def backward_body(wave, *refs):
    n = len(WAVES[wave])
    list_ref, vals_ref, grad_ref = refs[:3]
    outs, acc = refs[3:-1], refs[-1]
    acc[0:n] = jnp.zeros((n,) + acc.shape[1:], acc.dtype)
    feats = acc.shape[1]

    def multiply(entries, tiles):
        pieces = [grad_ref[:, column((e >> 9) & 31)] for e in entries]
        products = [
            jnp.dot(
                paired(pieces[u], pieces[u + 1]),
                jnp.concatenate([tiles[u], tiles[u + 1]], axis=0),
                preferred_element_type=jnp.float32,
            )
            for u in range(0, GROUP, 2)
        ]
        for u, e in enumerate(entries):
            half = products[u // 2][u % 2 * feats : (u % 2 + 1) * feats]
            acc[(e >> 20) + ((e >> 14) & 1) * n, :, column((e >> 15) & 31)] += half

    tile_loop(wave, list_ref, vals_ref, multiply)
    for j, out in enumerate(outs):
        out[...] = acc[j].astype(out.dtype)


def backward(wave, listed, vals, grad, dtypes):
    n = len(dtypes)
    return pl.pallas_call(
        functools.partial(backward_body, wave),
        out_shape=tuple(pltpu.VMEM(grad.shape, d) for d in dtypes),
        in_specs=[SMEM, VMEM, VMEM],
        out_specs=(VMEM,) * n,
        scratch_shapes=[pltpu.VMEM((n + 1,) + grad.shape, jnp.float32)],
        cost_estimate=COST,
        compiler_params=kept(8),
        name=f"backward_{wave}",
    )(listed, near(vals), near(grad))


def middle_body(factor, place_ref, *refs):
    ys, packed, (out_ref, grad_ref, wgrad_ref) = refs[0:4], refs[4:8], refs[8:]
    feats, nodes = ys[0].shape
    hidden = 4 * feats
    chunk = 512
    rows = []
    for k in range(4):
        w = packed[k][:, nodes:]
        rows.append(
            jnp.concatenate(
                [w[:, (j ^ k) * feats : ((j ^ k) + 1) * feats] for j in range(4)], axis=1
            )
        )
    own_rows = rows[0]
    turned = jnp.concatenate(rows, axis=0).T
    wgrad = jnp.zeros((feats, hidden), jnp.float32)
    for start in range(0, nodes, chunk):
        here = slice(start, start + chunk)
        y = jnp.concatenate([r[:, here] for r in ys], axis=0)
        pre = jnp.dot(turned, y, preferred_element_type=jnp.float32)
        sig = jax.nn.sigmoid(pre)
        out_ref[:, here] = (pre[:feats] * sig[:feats]).astype(out_ref.dtype)
        cot = jnp.concatenate([r[:, here] for r in packed], axis=0).astype(jnp.float32)
        grad_pre = (cot * (sig * (1.0 + pre * (1.0 - sig)))).astype(jnp.bfloat16)
        grad_ref[:, here] = jnp.dot(
            own_rows, grad_pre, preferred_element_type=jnp.float32
        ).astype(grad_ref.dtype)
        wgrad += lax.dot_general(
            ys[0][:, here], grad_pre, (((1,), (1,)), ((), ())), preferred_element_type=jnp.float32
        )
    wgrad_ref[...] = exchanged_columns(wgrad, place_ref[0]) * factor


def middle(place, ys, packed):
    feats, nodes = ys[0].shape
    factor = 1.0 / math.sqrt(nodes * lax.axis_size("blk"))
    return pl.pallas_call(
        functools.partial(middle_body, factor),
        out_shape=(
            jax.ShapeDtypeStruct((feats, nodes), jnp.bfloat16),
            pltpu.VMEM((feats, nodes), jnp.bfloat16),
            pltpu.VMEM((feats, 4 * feats), jnp.float32),
        ),
        in_specs=[SMEM] + [VMEM] * 8,
        out_specs=(VMEM,) * 3,
        cost_estimate=COST,
        compiler_params=kept(10),
        name="middle",
    )(place.astype(jnp.int32).reshape(1), *map(near, ys), *map(near, packed))


def fenced(*groups):
    return lax.optimization_barrier(groups)


def per_device(x_t, weight, cotangent, tile_row, tile_col, tile_off, tile_vals, tile_count):
    nodes = x_t.shape[1]
    f32, bf16 = jnp.float32, jnp.bfloat16
    place = lax.axis_index("feat")
    sign = (1 - 2 * (lax.axis_index("blk") % 2)).astype(jnp.int32).reshape(1)
    own = jnp.concatenate([cotangent, exchanged_columns(weight, place)], axis=1)

    x, u, v = flipped(x_t, "blk", 1), stepped(x_t, True), stepped(x_t, False)
    listed = plan(tile_row, tile_col, tile_off, tile_count, sign)
    x, u, v, listed, own = fenced(x, u, v, listed, own)
    m, n, far = stepped(u, True), stepped(v, False), flipped(own, "feat", 2)
    y = forward(0, listed, tile_vals, [x_t, u, v], None, f32)
    m, n, y, x = fenced(m, n, y, x)
    mx, xu, xv = flipped(m, "blk", 1), stepped(x, True), stepped(x, False)
    y = forward(1, listed, tile_vals, [x, m, n], y, f32)
    xu, xv, mx, y, far, own = fenced(xu, xv, mx, y, far, own)
    packed = [own, flipped(own, "feat", 1), far, flipped(far, "feat", 1)]
    y = forward(2, listed, tile_vals, [xu, xv, mx], y, bf16)
    y_far = flipped(y, "feat", 2)
    ys = [y, flipped(y, "feat", 1), y_far, flipped(y_far, "feat", 1)]
    out_t, grad, wgrad = middle(place, ys, packed)

    parts = [flipped(wgrad, "blk", bit) for bit in (2, 4, 6)]
    to_xu, to_xv, to_mx = backward(2, listed, tile_vals, grad, [bf16] * 3)
    to_xu, to_xv, to_mx, parts, grad = fenced(to_xu, to_xv, to_mx, parts, grad)
    from_mx, from_xu, from_xv = flipped(to_mx, "blk", 1), stepped(to_xu, False), stepped(to_xv, True)
    wgrad = (wgrad + parts[0]) + (parts[1] + parts[2])
    part = flipped(wgrad, "blk", 8)
    to_x, to_m, to_n = backward(1, listed, tile_vals, grad, [f32, f32, bf16])
    from_mx, from_xu, from_xv, to_m, to_n, to_x, grad, part = fenced(
        from_mx, from_xu, from_xv, to_m, to_n, to_x, grad, part
    )
    from_m = stepped((to_m + from_mx.astype(f32)).astype(bf16), False)
    from_n = stepped(to_n, True)
    total, to_u, to_v = backward(0, listed, tile_vals, grad, [f32] * 3)
    from_x = flipped((to_x + from_xu.astype(f32) + from_xv.astype(f32)).astype(bf16), "blk", 1)
    wgrad = wgrad + part
    part = flipped(wgrad, "blk", 16)
    total, to_u, to_v, part = fenced(total, to_u, to_v, part)
    wgrad = wgrad + part
    part = flipped(wgrad, "blk", 32)
    from_m, from_n, to_u, to_v, part = fenced(from_m, from_n, to_u, to_v, part)
    wgrad = wgrad + part
    part = flipped(wgrad, "blk", 1)
    from_u = stepped((to_u + from_m.astype(f32)).astype(bf16), False)
    from_v = stepped((to_v + from_n.astype(f32)).astype(bf16), True)
    wgrad = wgrad + part
    total = total + from_u.astype(f32) + from_v.astype(f32) + from_x.astype(f32)
    return (out_t, total.astype(bf16), wgrad)


def solution(mesh):
    placed = (
        P("feat", "blk"),
        P("feat", None),
        P("feat", "blk"),
        P("blk"),
        P("blk"),
        P("blk"),
        P("blk", None, None),
        P("blk"),
    )
    return jax.shard_map(
        per_device,
        mesh=mesh,
        in_specs=placed,
        out_specs=(P("feat", "blk"), P("feat", "blk"), P("feat", None)),
        check_vma=False,
    )
```

```python
import functools
import math

import jax
import jax.numpy as jnp
from jax import lax
from jax.experimental import pallas as pl
from jax.experimental.pallas import tpu as pltpu
from jax.sharding import PartitionSpec as P

REACH = 4
GROUP = 8
WAVES = [[0, 2, -2], [1, 4, -4], [3, -1, -3]]
MIB = 1 << 20


def stepped(block, forth):
    count = lax.axis_size("blk")
    route = [((i + (2 if forth == (i % 2 == 0) else -2)) % count, i) for i in range(count)]
    return lax.ppermute(block, "blk", route)


def flipped(block, axis, bit):
    return lax.ppermute(block, axis, [(i, i ^ bit) for i in range(lax.axis_size(axis))])


def exchanged_columns(array, place):
    q = array.shape[1] // 4
    b = [array[:, i * q : (i + 1) * q] for i in range(4)]
    swapped = jnp.concatenate([b[1], b[0], b[3], b[2]], axis=1)
    array = jnp.where(place % 2 == 1, swapped, array)
    halves = jnp.concatenate([array[:, 2 * q :], array[:, : 2 * q]], axis=1)
    return jnp.where(place // 2 == 1, halves, array)


COST = pl.CostEstimate(flops=0, transcendentals=0, bytes_accessed=6_000_000)
SMEM = pl.BlockSpec(memory_space=pltpu.SMEM)
VMEM = pl.BlockSpec(memory_space=pltpu.VMEM)


def near(array):
    return pltpu.with_memory_space_constraint(array, pltpu.VMEM)


def kept(mib):
    return pltpu.CompilerParams(vmem_limit_bytes=mib * MIB)


def plan_body(cap, row_ref, col_ref, off_ref, count_ref, sign_ref, list_ref, fill, home):
    sign = sign_ref[0]
    for w, wave in enumerate(WAVES):
        fill[w] = 0
        for j, offset in enumerate(wave):
            home[offset + REACH] = w + 16 * j

    def place(s, c):
        at_home = home[off_ref[s] * sign + REACH]
        wave = at_home & 15
        n = fill[wave]
        fill[wave] = n + 1
        list_ref[wave * cap + n] = (
            s + (row_ref[s] << 9) + (col_ref[s] << 15) + ((at_home >> 4) << 20)
        )
        return c

    lax.fori_loop(0, count_ref[0], place, 0)
    for w in range(len(WAVES)):
        n = fill[w]
        groups = (n + GROUP - 1) >> 3

        def pad(i, c):
            list_ref[w * cap + i] = 32 << 9
            return c

        lax.fori_loop(n, groups * GROUP, pad, 0)
        list_ref[len(WAVES) * cap + w] = groups


def plan(tile_row, tile_col, tile_off, tile_count, sign):
    cap = tile_row.shape[0] + GROUP
    return pl.pallas_call(
        functools.partial(plan_body, cap),
        out_shape=jax.ShapeDtypeStruct((len(WAVES) * cap + 16,), jnp.int32),
        in_specs=[SMEM] * 5,
        out_specs=SMEM,
        scratch_shapes=[pltpu.SMEM((16,), jnp.int32)] * 2,
        cost_estimate=COST,
        compiler_params=kept(2),
        name="plan",
    )(tile_row, tile_col, tile_off, tile_count, sign)


def tile_loop(wave, list_ref, vals_ref, multiply):
    cap = (list_ref.shape[0] - 16) // len(WAVES)

    def body(g, c):
        entries = [list_ref[wave * cap + g * GROUP + u] for u in range(GROUP)]
        multiply(entries, [vals_ref[e & 511] for e in entries])
        return c

    lax.fori_loop(0, list_ref[len(WAVES) * cap + wave], body, 0)


def column(tile):
    return pl.ds(pl.multiple_of(tile * 128, 128), 128)


def paired(first, second):
    zero = jnp.zeros_like(first)
    return jnp.concatenate(
        [jnp.concatenate([first, zero], axis=1), jnp.concatenate([zero, second], axis=1)], axis=0
    )


def forward_body(wave, seeded, *refs):
    n = len(WAVES[wave])
    list_ref, vals_ref = refs[:2]
    slabs, rest = refs[2 : 2 + n], refs[2 + n :]
    if seeded:
        seed_ref, rest = rest[0], rest[1:]
    out_ref, held = rest[:2]
    acc = rest[2] if len(rest) > 2 else out_ref
    acc[...] = seed_ref[...] if seeded else jnp.zeros_like(acc)
    for j, slab in enumerate(slabs):
        held[j] = slab[...]
    feats = acc.shape[0]
    held[n, :, 0:128] = jnp.zeros((feats, 128), held.dtype)

    def multiply(entries, tiles):
        pieces = [
            held[(e >> 20) + ((e >> 14) & 1) * n, :, column((e >> 15) & 31)] for e in entries
        ]
        products = [
            lax.dot_general(
                paired(pieces[u], pieces[u + 1]),
                jnp.concatenate([tiles[u], tiles[u + 1]], axis=1),
                (((1,), (1,)), ((), ())),
                preferred_element_type=jnp.float32,
            )
            for u in range(0, GROUP, 2)
        ]
        for u, e in enumerate(entries):
            half = products[u // 2][u % 2 * feats : (u % 2 + 1) * feats]
            acc[:, column((e >> 9) & 31)] += half

    tile_loop(wave, list_ref, vals_ref, multiply)
    if acc is not out_ref:
        out_ref[...] = acc[...].astype(out_ref.dtype)


def forward(wave, listed, vals, slabs, seed, dtype):
    feats, nodes = slabs[0].shape
    wide = dtype == jnp.float32
    return pl.pallas_call(
        functools.partial(forward_body, wave, seed is not None),
        out_shape=pltpu.VMEM((feats, nodes), dtype),
        in_specs=[SMEM] + [VMEM] * (1 + len(slabs) + (seed is not None)),
        out_specs=VMEM,
        scratch_shapes=[pltpu.VMEM((len(slabs) + 1, feats, nodes), slabs[0].dtype)]
        + ([] if wide else [pltpu.VMEM((feats, nodes), jnp.float32)]),
        cost_estimate=COST,
        compiler_params=kept(8),
        name=f"forward_{wave}",
    )(listed, near(vals), *map(near, slabs), *(() if seed is None else (near(seed),)))


def backward_body(wave, *refs):
    n = len(WAVES[wave])
    list_ref, vals_ref, grad_ref = refs[:3]
    outs, acc = refs[3:-1], refs[-1]
    acc[0:n] = jnp.zeros((n,) + acc.shape[1:], acc.dtype)
    feats = acc.shape[1]

    def multiply(entries, tiles):
        pieces = [grad_ref[:, column((e >> 9) & 31)] for e in entries]
        products = [
            jnp.dot(
                paired(pieces[u], pieces[u + 1]),
                jnp.concatenate([tiles[u], tiles[u + 1]], axis=0),
                preferred_element_type=jnp.float32,
            )
            for u in range(0, GROUP, 2)
        ]
        for u, e in enumerate(entries):
            half = products[u // 2][u % 2 * feats : (u % 2 + 1) * feats]
            acc[(e >> 20) + ((e >> 14) & 1) * n, :, column((e >> 15) & 31)] += half

    tile_loop(wave, list_ref, vals_ref, multiply)
    for j, out in enumerate(outs):
        out[...] = acc[j].astype(out.dtype)


def backward(wave, listed, vals, grad, dtypes):
    n = len(dtypes)
    return pl.pallas_call(
        functools.partial(backward_body, wave),
        out_shape=tuple(pltpu.VMEM(grad.shape, d) for d in dtypes),
        in_specs=[SMEM, VMEM, VMEM],
        out_specs=(VMEM,) * n,
        scratch_shapes=[pltpu.VMEM((n + 1,) + grad.shape, jnp.float32)],
        cost_estimate=COST,
        compiler_params=kept(8),
        name=f"backward_{wave}",
    )(listed, near(vals), near(grad))


def middle_body(factor, place_ref, *refs):
    ys, packed, (out_ref, grad_ref, wgrad_ref) = refs[0:4], refs[4:8], refs[8:]
    feats, nodes = ys[0].shape
    hidden = 4 * feats
    chunk = 512
    rows = []
    for k in range(4):
        w = packed[k][:, nodes:]
        rows.append(
            jnp.concatenate(
                [w[:, (j ^ k) * feats : ((j ^ k) + 1) * feats] for j in range(4)], axis=1
            )
        )
    own_rows = rows[0]
    turned = jnp.concatenate(rows, axis=0).T
    wgrad = jnp.zeros((feats, hidden), jnp.float32)
    for start in range(0, nodes, chunk):
        here = slice(start, start + chunk)
        y = jnp.concatenate([r[:, here] for r in ys], axis=0)
        pre = jnp.dot(turned, y, preferred_element_type=jnp.float32)
        sig = jax.nn.sigmoid(pre)
        out_ref[:, here] = (pre[:feats] * sig[:feats]).astype(out_ref.dtype)
        cot = jnp.concatenate([r[:, here] for r in packed], axis=0).astype(jnp.float32)
        grad_pre = (cot * (sig * (1.0 + pre * (1.0 - sig)))).astype(jnp.bfloat16)
        grad_ref[:, here] = jnp.dot(
            own_rows, grad_pre, preferred_element_type=jnp.float32
        ).astype(grad_ref.dtype)
        wgrad += lax.dot_general(
            ys[0][:, here], grad_pre, (((1,), (1,)), ((), ())), preferred_element_type=jnp.float32
        )
    wgrad_ref[...] = exchanged_columns(wgrad, place_ref[0]) * factor


def middle(place, ys, packed):
    feats, nodes = ys[0].shape
    factor = 1.0 / math.sqrt(nodes * lax.axis_size("blk"))
    return pl.pallas_call(
        functools.partial(middle_body, factor),
        out_shape=(
            jax.ShapeDtypeStruct((feats, nodes), jnp.bfloat16),
            pltpu.VMEM((feats, nodes), jnp.bfloat16),
            pltpu.VMEM((feats, 4 * feats), jnp.float32),
        ),
        in_specs=[SMEM] + [VMEM] * 8,
        out_specs=(VMEM,) * 3,
        cost_estimate=COST,
        compiler_params=kept(10),
        name="middle",
    )(place.astype(jnp.int32).reshape(1), *map(near, ys), *map(near, packed))


def fenced(*groups):
    return lax.optimization_barrier(groups)


def per_device(x_t, weight, cotangent, tile_row, tile_col, tile_off, tile_vals, tile_count):
    nodes = x_t.shape[1]
    f32, bf16 = jnp.float32, jnp.bfloat16
    place = lax.axis_index("feat")
    sign = (1 - 2 * (lax.axis_index("blk") % 2)).astype(jnp.int32).reshape(1)
    own = jnp.concatenate([cotangent, exchanged_columns(weight, place)], axis=1)

    x, u, v = flipped(x_t, "blk", 1), stepped(x_t, True), stepped(x_t, False)
    listed = plan(tile_row, tile_col, tile_off, tile_count, sign)
    x, u, v, listed, own = fenced(x, u, v, listed, own)
    m, n, far = stepped(u, True), stepped(v, False), flipped(own, "feat", 2)
    y = forward(0, listed, tile_vals, [x_t, u, v], None, f32)
    m, n, y, x = fenced(m, n, y, x)
    mx, xu, xv = flipped(m, "blk", 1), stepped(x, True), stepped(x, False)
    y = forward(1, listed, tile_vals, [x, m, n], y, f32)
    xu, xv, mx, y, far, own = fenced(xu, xv, mx, y, far, own)
    packed = [own, flipped(own, "feat", 1), far, flipped(far, "feat", 1)]
    y = forward(2, listed, tile_vals, [xu, xv, mx], y, bf16)
    y_far = flipped(y, "feat", 2)
    ys = [y, flipped(y, "feat", 1), y_far, flipped(y_far, "feat", 1)]
    out_t, grad, wgrad = middle(place, ys, packed)

    to_xu, to_xv, to_mx = backward(2, listed, tile_vals, grad, [bf16] * 3)
    to_xu, to_xv, to_mx, wgrad, grad = fenced(to_xu, to_xv, to_mx, wgrad, grad)
    from_mx, from_xu, from_xv = flipped(to_mx, "blk", 1), stepped(to_xu, False), stepped(to_xv, True)
    part = flipped(wgrad, "blk", 8)
    to_x, to_m, to_n = backward(1, listed, tile_vals, grad, [f32, f32, bf16])
    part, to_m, to_x = fenced(part, to_m, to_x)
    wgrad = wgrad + part
    part = flipped(wgrad, "blk", 2)
    from_mx, from_xu, from_xv, to_m, to_n, to_x, grad, part = fenced(
        from_mx, from_xu, from_xv, to_m, to_n, to_x, grad, part
    )
    from_m = stepped((to_m + from_mx.astype(f32)).astype(bf16), False)
    from_n = stepped(to_n, True)
    total, to_u, to_v = backward(0, listed, tile_vals, grad, [f32] * 3)
    from_x = flipped((to_x + from_xu.astype(f32) + from_xv.astype(f32)).astype(bf16), "blk", 1)
    wgrad = wgrad + part
    part = flipped(wgrad, "blk", 16)
    total, to_u, to_v, part = fenced(total, to_u, to_v, part)
    wgrad = wgrad + part
    part = flipped(wgrad, "blk", 4)
    from_m, from_n, to_u, to_v, part = fenced(from_m, from_n, to_u, to_v, part)
    wgrad = wgrad + part
    wgrad = wgrad + flipped(wgrad, "blk", 32)
    part = flipped(wgrad, "blk", 1)
    from_u = stepped((to_u + from_m.astype(f32)).astype(bf16), False)
    from_v = stepped((to_v + from_n.astype(f32)).astype(bf16), True)
    wgrad = wgrad + part
    total = total + from_u.astype(f32) + from_v.astype(f32) + from_x.astype(f32)
    return (out_t, total.astype(bf16), wgrad)


def solution(mesh):
    placed = (
        P("feat", "blk"),
        P("feat", None),
        P("feat", "blk"),
        P("blk"),
        P("blk"),
        P("blk"),
        P("blk", None, None),
        P("blk"),
    )
    return jax.shard_map(
        per_device,
        mesh=mesh,
        in_specs=placed,
        out_specs=(P("feat", "blk"), P("feat", "blk"), P("feat", None)),
        check_vma=False,
    )
```

```python
import functools
import math

import jax
import jax.numpy as jnp
from jax import lax
from jax.experimental import pallas as pl
from jax.experimental.pallas import tpu as pltpu
from jax.sharding import PartitionSpec as P

REACH = 4
GROUP = 8
WAVES = [[0, 2, -2], [1, 4, -4], [3, -1, -3]]
MIB = 1 << 20


def stepped(block, forth):
    count = lax.axis_size("blk")
    route = [((i + (2 if forth == (i % 2 == 0) else -2)) % count, i) for i in range(count)]
    return lax.ppermute(block, "blk", route)


def flipped(block, axis, bit):
    return lax.ppermute(block, axis, [(i, i ^ bit) for i in range(lax.axis_size(axis))])


def exchanged_columns(array, place):
    q = array.shape[1] // 4
    b = [array[:, i * q : (i + 1) * q] for i in range(4)]
    swapped = jnp.concatenate([b[1], b[0], b[3], b[2]], axis=1)
    array = jnp.where(place % 2 == 1, swapped, array)
    halves = jnp.concatenate([array[:, 2 * q :], array[:, : 2 * q]], axis=1)
    return jnp.where(place // 2 == 1, halves, array)


COST = pl.CostEstimate(flops=0, transcendentals=0, bytes_accessed=6_000_000)
SMEM = pl.BlockSpec(memory_space=pltpu.SMEM)
VMEM = pl.BlockSpec(memory_space=pltpu.VMEM)


def near(array):
    return pltpu.with_memory_space_constraint(array, pltpu.VMEM)


def kept(mib):
    return pltpu.CompilerParams(vmem_limit_bytes=mib * MIB)


def plan_body(cap, row_ref, col_ref, off_ref, count_ref, sign_ref, list_ref, fill, home):
    sign = sign_ref[0]
    for w, wave in enumerate(WAVES):
        fill[w] = 0
        for j, offset in enumerate(wave):
            home[offset + REACH] = w + 16 * j

    def place(s, c):
        at_home = home[off_ref[s] * sign + REACH]
        wave = at_home & 15
        n = fill[wave]
        fill[wave] = n + 1
        list_ref[wave * cap + n] = (
            s + (row_ref[s] << 9) + (col_ref[s] << 15) + ((at_home >> 4) << 20)
        )
        return c

    lax.fori_loop(0, count_ref[0], place, 0)
    for w in range(len(WAVES)):
        n = fill[w]
        groups = (n + GROUP - 1) >> 3

        def pad(i, c):
            list_ref[w * cap + i] = 32 << 9
            return c

        lax.fori_loop(n, groups * GROUP, pad, 0)
        list_ref[len(WAVES) * cap + w] = groups


def plan(tile_row, tile_col, tile_off, tile_count, sign):
    cap = tile_row.shape[0] + GROUP
    return pl.pallas_call(
        functools.partial(plan_body, cap),
        out_shape=jax.ShapeDtypeStruct((len(WAVES) * cap + 16,), jnp.int32),
        in_specs=[SMEM] * 5,
        out_specs=SMEM,
        scratch_shapes=[pltpu.SMEM((16,), jnp.int32)] * 2,
        cost_estimate=COST,
        compiler_params=kept(2),
        name="plan",
    )(tile_row, tile_col, tile_off, tile_count, sign)


def tile_loop(wave, list_ref, vals_ref, multiply):
    cap = (list_ref.shape[0] - 16) // len(WAVES)

    def body(g, c):
        entries = [list_ref[wave * cap + g * GROUP + u] for u in range(GROUP)]
        multiply(entries, [vals_ref[e & 511] for e in entries])
        return c

    lax.fori_loop(0, list_ref[len(WAVES) * cap + wave], body, 0)


def column(tile):
    return pl.ds(pl.multiple_of(tile * 128, 128), 128)


def paired(first, second):
    zero = jnp.zeros_like(first)
    return jnp.concatenate(
        [jnp.concatenate([first, zero], axis=1), jnp.concatenate([zero, second], axis=1)], axis=0
    )


def forward_body(wave, seeded, *refs):
    n = len(WAVES[wave])
    list_ref, vals_ref = refs[:2]
    slabs, rest = refs[2 : 2 + n], refs[2 + n :]
    if seeded:
        seed_ref, rest = rest[0], rest[1:]
    out_ref, held = rest[:2]
    acc = rest[2] if len(rest) > 2 else out_ref
    acc[...] = seed_ref[...] if seeded else jnp.zeros_like(acc)
    for j, slab in enumerate(slabs):
        held[j] = slab[...]
    feats = acc.shape[0]
    held[n, :, 0:128] = jnp.zeros((feats, 128), held.dtype)

    def multiply(entries, tiles):
        pieces = [
            held[(e >> 20) + ((e >> 14) & 1) * n, :, column((e >> 15) & 31)] for e in entries
        ]
        products = [
            lax.dot_general(
                paired(pieces[u], pieces[u + 1]),
                jnp.concatenate([tiles[u], tiles[u + 1]], axis=1),
                (((1,), (1,)), ((), ())),
                preferred_element_type=jnp.float32,
            )
            for u in range(0, GROUP, 2)
        ]
        for u, e in enumerate(entries):
            half = products[u // 2][u % 2 * feats : (u % 2 + 1) * feats]
            acc[:, column((e >> 9) & 31)] += half

    tile_loop(wave, list_ref, vals_ref, multiply)
    if acc is not out_ref:
        out_ref[...] = acc[...].astype(out_ref.dtype)


def forward(wave, listed, vals, slabs, seed, dtype):
    feats, nodes = slabs[0].shape
    wide = dtype == jnp.float32
    return pl.pallas_call(
        functools.partial(forward_body, wave, seed is not None),
        out_shape=pltpu.VMEM((feats, nodes), dtype),
        in_specs=[SMEM] + [VMEM] * (1 + len(slabs) + (seed is not None)),
        out_specs=VMEM,
        scratch_shapes=[pltpu.VMEM((len(slabs) + 1, feats, nodes), slabs[0].dtype)]
        + ([] if wide else [pltpu.VMEM((feats, nodes), jnp.float32)]),
        cost_estimate=COST,
        compiler_params=kept(8),
        name=f"forward_{wave}",
    )(listed, near(vals), *map(near, slabs), *(() if seed is None else (near(seed),)))


def backward_body(wave, *refs):
    n = len(WAVES[wave])
    list_ref, vals_ref, grad_ref = refs[:3]
    outs, acc = refs[3:-1], refs[-1]
    acc[0:n] = jnp.zeros((n,) + acc.shape[1:], acc.dtype)
    feats = acc.shape[1]

    def multiply(entries, tiles):
        pieces = [grad_ref[:, column((e >> 9) & 31)] for e in entries]
        products = [
            jnp.dot(
                paired(pieces[u], pieces[u + 1]),
                jnp.concatenate([tiles[u], tiles[u + 1]], axis=0),
                preferred_element_type=jnp.float32,
            )
            for u in range(0, GROUP, 2)
        ]
        for u, e in enumerate(entries):
            half = products[u // 2][u % 2 * feats : (u % 2 + 1) * feats]
            acc[(e >> 20) + ((e >> 14) & 1) * n, :, column((e >> 15) & 31)] += half

    tile_loop(wave, list_ref, vals_ref, multiply)
    for j, out in enumerate(outs):
        out[...] = acc[j].astype(out.dtype)


def backward(wave, listed, vals, grad, dtypes):
    n = len(dtypes)
    return pl.pallas_call(
        functools.partial(backward_body, wave),
        out_shape=tuple(pltpu.VMEM(grad.shape, d) for d in dtypes),
        in_specs=[SMEM, VMEM, VMEM],
        out_specs=(VMEM,) * n,
        scratch_shapes=[pltpu.VMEM((n + 1,) + grad.shape, jnp.float32)],
        cost_estimate=COST,
        compiler_params=kept(8),
        name=f"backward_{wave}",
    )(listed, near(vals), near(grad))


def middle_body(factor, place_ref, *refs):
    ys, packed, (out_ref, grad_ref, wgrad_ref) = refs[0:4], refs[4:8], refs[8:]
    feats, nodes = ys[0].shape
    hidden = 4 * feats
    chunk = 512
    rows = []
    for k in range(4):
        w = packed[k][:, nodes:]
        rows.append(
            jnp.concatenate(
                [w[:, (j ^ k) * feats : ((j ^ k) + 1) * feats] for j in range(4)], axis=1
            )
        )
    own_rows = rows[0]
    turned = jnp.concatenate(rows, axis=0).T
    wgrad = jnp.zeros((feats, hidden), jnp.float32)
    for start in range(0, nodes, chunk):
        here = slice(start, start + chunk)
        y = jnp.concatenate([r[:, here] for r in ys], axis=0)
        pre = jnp.dot(turned, y, preferred_element_type=jnp.float32)
        sig = jax.nn.sigmoid(pre)
        out_ref[:, here] = (pre[:feats] * sig[:feats]).astype(out_ref.dtype)
        cot = jnp.concatenate([r[:, here] for r in packed], axis=0).astype(jnp.float32)
        grad_pre = (cot * (sig * (1.0 + pre * (1.0 - sig)))).astype(jnp.bfloat16)
        grad_ref[:, here] = jnp.dot(
            own_rows, grad_pre, preferred_element_type=jnp.float32
        ).astype(grad_ref.dtype)
        wgrad += lax.dot_general(
            ys[0][:, here], grad_pre, (((1,), (1,)), ((), ())), preferred_element_type=jnp.float32
        )
    wgrad_ref[...] = exchanged_columns(wgrad, place_ref[0]) * factor


def middle(place, ys, packed):
    feats, nodes = ys[0].shape
    factor = 1.0 / math.sqrt(nodes * lax.axis_size("blk"))
    return pl.pallas_call(
        functools.partial(middle_body, factor),
        out_shape=(
            jax.ShapeDtypeStruct((feats, nodes), jnp.bfloat16),
            pltpu.VMEM((feats, nodes), jnp.bfloat16),
            pltpu.VMEM((feats, 4 * feats), jnp.float32),
        ),
        in_specs=[SMEM] + [VMEM] * 8,
        out_specs=(VMEM,) * 3,
        cost_estimate=COST,
        compiler_params=kept(10),
        name="middle",
    )(place.astype(jnp.int32).reshape(1), *map(near, ys), *map(near, packed))


def fenced(*groups):
    return lax.optimization_barrier(groups)


def per_device(x_t, weight, cotangent, tile_row, tile_col, tile_off, tile_vals, tile_count):
    nodes = x_t.shape[1]
    f32, bf16 = jnp.float32, jnp.bfloat16
    place = lax.axis_index("feat")
    sign = (1 - 2 * (lax.axis_index("blk") % 2)).astype(jnp.int32).reshape(1)
    own = jnp.concatenate([cotangent, exchanged_columns(weight, place)], axis=1)

    x, u, v = flipped(x_t, "blk", 1), stepped(x_t, True), stepped(x_t, False)
    listed = plan(tile_row, tile_col, tile_off, tile_count, sign)
    x, u, v, listed, own = fenced(x, u, v, listed, own)
    m, n, far = stepped(u, True), stepped(v, False), flipped(own, "feat", 2)
    y = forward(0, listed, tile_vals, [x_t, u, v], None, f32)
    m, n, y, x = fenced(m, n, y, x)
    mx, xu, xv = flipped(m, "blk", 1), stepped(x, True), stepped(x, False)
    y = forward(1, listed, tile_vals, [x, m, n], y, f32)
    xu, xv, mx, y, far, own = fenced(xu, xv, mx, y, far, own)
    packed = [own, flipped(own, "feat", 1), far, flipped(far, "feat", 1)]
    y = forward(2, listed, tile_vals, [xu, xv, mx], y, bf16)
    y_far = flipped(y, "feat", 2)
    ys = [y, flipped(y, "feat", 1), y_far, flipped(y_far, "feat", 1)]
    out_t, grad, wgrad = middle(place, ys, packed)

    part = flipped(wgrad, "blk", 2)
    to_xu, to_xv, to_mx = backward(2, listed, tile_vals, grad, [bf16] * 3)
    to_xu, to_xv, to_mx, part, grad = fenced(to_xu, to_xv, to_mx, part, grad)
    from_mx, from_xu, from_xv = flipped(to_mx, "blk", 1), stepped(to_xu, False), stepped(to_xv, True)
    wgrad = wgrad + part
    part = flipped(wgrad, "blk", 8)
    to_x, to_m, to_n = backward(1, listed, tile_vals, grad, [f32, f32, bf16])
    part, to_m, grad = fenced(part, to_m, grad)
    wgrad = wgrad + part
    part = flipped(wgrad, "blk", 16)
    total, to_u, to_v = backward(0, listed, tile_vals, grad, [f32] * 3)
    from_mx, from_xu, from_xv, to_m, to_n, total, to_x, to_u, to_v, part = fenced(
        from_mx, from_xu, from_xv, to_m, to_n, total, to_x, to_u, to_v, part
    )
    from_m = stepped((to_m + from_mx.astype(f32)).astype(bf16), False)
    from_n = stepped(to_n, True)
    to_x = (to_x + from_xu.astype(f32) + from_xv.astype(f32)).astype(bf16)
    wgrad = wgrad + part
    wgrad = wgrad + flipped(wgrad, "blk", 48)
    wgrad = wgrad + flipped(wgrad, "blk", 1)
    from_m, from_n, to_x, to_u, to_v, wgrad = fenced(from_m, from_n, to_x, to_u, to_v, wgrad)
    part = flipped(wgrad, "blk", 6)
    from_u = stepped((to_u + from_m.astype(f32)).astype(bf16), False)
    from_v = stepped((to_v + from_n.astype(f32)).astype(bf16), True)
    from_x = flipped(to_x, "blk", 1)
    wgrad = wgrad + part
    total = total + from_u.astype(f32) + from_v.astype(f32) + from_x.astype(f32)
    return (out_t, total.astype(bf16), wgrad)


def solution(mesh):
    placed = (
        P("feat", "blk"),
        P("feat", None),
        P("feat", "blk"),
        P("blk"),
        P("blk"),
        P("blk"),
        P("blk", None, None),
        P("blk"),
    )
    return jax.shard_map(
        per_device,
        mesh=mesh,
        in_specs=placed,
        out_specs=(P("feat", "blk"), P("feat", "blk"), P("feat", None)),
        check_vma=False,
    )
```

```python
import functools
import math

import jax
import jax.numpy as jnp
from jax import lax
from jax.experimental import pallas as pl
from jax.experimental.pallas import tpu as pltpu
from jax.sharding import PartitionSpec as P

REACH = 4
GROUP = 16
WAVES = [[0, 2, -2], [1, 4, -4], [3, -1, -3]]
MIB = 1 << 20


def stepped(block, forth):
    count = lax.axis_size("blk")
    route = [((i + (2 if forth == (i % 2 == 0) else -2)) % count, i) for i in range(count)]
    return lax.ppermute(block, "blk", route)


def flipped(block, axis, bit):
    return lax.ppermute(block, axis, [(i, i ^ bit) for i in range(lax.axis_size(axis))])


def exchanged_columns(array, place):
    q = array.shape[1] // 4
    b = [array[:, i * q : (i + 1) * q] for i in range(4)]
    swapped = jnp.concatenate([b[1], b[0], b[3], b[2]], axis=1)
    array = jnp.where(place % 2 == 1, swapped, array)
    halves = jnp.concatenate([array[:, 2 * q :], array[:, : 2 * q]], axis=1)
    return jnp.where(place // 2 == 1, halves, array)


COST = pl.CostEstimate(flops=0, transcendentals=0, bytes_accessed=6_000_000)
SMEM = pl.BlockSpec(memory_space=pltpu.SMEM)
VMEM = pl.BlockSpec(memory_space=pltpu.VMEM)


def near(array):
    return pltpu.with_memory_space_constraint(array, pltpu.VMEM)


def kept(mib):
    return pltpu.CompilerParams(vmem_limit_bytes=mib * MIB)


def plan_body(cap, row_ref, col_ref, off_ref, count_ref, sign_ref, list_ref, fill, home):
    sign = sign_ref[0]
    for w, wave in enumerate(WAVES):
        fill[w] = 0
        for j, offset in enumerate(wave):
            home[offset + REACH] = w + 16 * j

    def place(s, c):
        at_home = home[off_ref[s] * sign + REACH]
        wave = at_home & 15
        n = fill[wave]
        fill[wave] = n + 1
        list_ref[wave * cap + n] = (
            s + (row_ref[s] << 9) + (col_ref[s] << 15) + ((at_home >> 4) << 20)
        )
        return c

    lax.fori_loop(0, count_ref[0], place, 0)
    for w in range(len(WAVES)):
        n = fill[w]
        groups = (n + GROUP - 1) >> 4

        def pad(i, c):
            list_ref[w * cap + i] = 32 << 9
            return c

        lax.fori_loop(n, groups * GROUP, pad, 0)
        list_ref[len(WAVES) * cap + w] = groups


def plan(tile_row, tile_col, tile_off, tile_count, sign):
    cap = tile_row.shape[0] + GROUP
    return pl.pallas_call(
        functools.partial(plan_body, cap),
        out_shape=jax.ShapeDtypeStruct((len(WAVES) * cap + 16,), jnp.int32),
        in_specs=[SMEM] * 5,
        out_specs=SMEM,
        scratch_shapes=[pltpu.SMEM((16,), jnp.int32)] * 2,
        cost_estimate=COST,
        compiler_params=kept(2),
        name="plan",
    )(tile_row, tile_col, tile_off, tile_count, sign)


def tile_loop(wave, list_ref, vals_ref, multiply):
    cap = (list_ref.shape[0] - 16) // len(WAVES)

    def body(g, c):
        entries = [list_ref[wave * cap + g * GROUP + u] for u in range(GROUP)]
        multiply(entries, [vals_ref[e & 511] for e in entries])
        return c

    lax.fori_loop(0, list_ref[len(WAVES) * cap + wave], body, 0)


def column(tile):
    return pl.ds(pl.multiple_of(tile * 128, 128), 128)


def paired(first, second):
    zero = jnp.zeros_like(first)
    return jnp.concatenate(
        [jnp.concatenate([first, zero], axis=1), jnp.concatenate([zero, second], axis=1)], axis=0
    )


def forward_body(wave, seeded, *refs):
    n = len(WAVES[wave])
    list_ref, vals_ref = refs[:2]
    slabs, rest = refs[2 : 2 + n], refs[2 + n :]
    if seeded:
        seed_ref, rest = rest[0], rest[1:]
    out_ref, held = rest[:2]
    acc = rest[2] if len(rest) > 2 else out_ref
    acc[...] = seed_ref[...] if seeded else jnp.zeros_like(acc)
    for j, slab in enumerate(slabs):
        held[j] = slab[...]
    feats = acc.shape[0]
    held[n, :, 0:128] = jnp.zeros((feats, 128), held.dtype)

    def multiply(entries, tiles):
        pieces = [
            held[(e >> 20) + ((e >> 14) & 1) * n, :, column((e >> 15) & 31)] for e in entries
        ]
        products = [
            lax.dot_general(
                paired(pieces[u], pieces[u + 1]),
                jnp.concatenate([tiles[u], tiles[u + 1]], axis=1),
                (((1,), (1,)), ((), ())),
                preferred_element_type=jnp.float32,
            )
            for u in range(0, GROUP, 2)
        ]
        for u, e in enumerate(entries):
            half = products[u // 2][u % 2 * feats : (u % 2 + 1) * feats]
            acc[:, column((e >> 9) & 31)] += half

    tile_loop(wave, list_ref, vals_ref, multiply)
    if acc is not out_ref:
        out_ref[...] = acc[...].astype(out_ref.dtype)


def forward(wave, listed, vals, slabs, seed, dtype):
    feats, nodes = slabs[0].shape
    wide = dtype == jnp.float32
    return pl.pallas_call(
        functools.partial(forward_body, wave, seed is not None),
        out_shape=pltpu.VMEM((feats, nodes), dtype),
        in_specs=[SMEM] + [VMEM] * (1 + len(slabs) + (seed is not None)),
        out_specs=VMEM,
        scratch_shapes=[pltpu.VMEM((len(slabs) + 1, feats, nodes), slabs[0].dtype)]
        + ([] if wide else [pltpu.VMEM((feats, nodes), jnp.float32)]),
        cost_estimate=COST,
        compiler_params=kept(8),
        name=f"forward_{wave}",
    )(listed, near(vals), *map(near, slabs), *(() if seed is None else (near(seed),)))


def backward_body(wave, *refs):
    n = len(WAVES[wave])
    list_ref, vals_ref, grad_ref = refs[:3]
    outs, acc = refs[3:-1], refs[-1]
    acc[0:n] = jnp.zeros((n,) + acc.shape[1:], acc.dtype)
    feats = acc.shape[1]

    def multiply(entries, tiles):
        pieces = [grad_ref[:, column((e >> 9) & 31)] for e in entries]
        products = [
            jnp.dot(
                paired(pieces[u], pieces[u + 1]),
                jnp.concatenate([tiles[u], tiles[u + 1]], axis=0),
                preferred_element_type=jnp.float32,
            )
            for u in range(0, GROUP, 2)
        ]
        for u, e in enumerate(entries):
            half = products[u // 2][u % 2 * feats : (u % 2 + 1) * feats]
            acc[(e >> 20) + ((e >> 14) & 1) * n, :, column((e >> 15) & 31)] += half

    tile_loop(wave, list_ref, vals_ref, multiply)
    for j, out in enumerate(outs):
        out[...] = acc[j].astype(out.dtype)


def backward(wave, listed, vals, grad, dtypes):
    n = len(dtypes)
    return pl.pallas_call(
        functools.partial(backward_body, wave),
        out_shape=tuple(pltpu.VMEM(grad.shape, d) for d in dtypes),
        in_specs=[SMEM, VMEM, VMEM],
        out_specs=(VMEM,) * n,
        scratch_shapes=[pltpu.VMEM((n + 1,) + grad.shape, jnp.float32)],
        cost_estimate=COST,
        compiler_params=kept(8),
        name=f"backward_{wave}",
    )(listed, near(vals), near(grad))


def middle_body(factor, place_ref, *refs):
    ys, packed, (out_ref, grad_ref, wgrad_ref) = refs[0:4], refs[4:8], refs[8:]
    feats, nodes = ys[0].shape
    hidden = 4 * feats
    chunk = 512
    rows = []
    for k in range(4):
        w = packed[k][:, nodes:]
        rows.append(
            jnp.concatenate(
                [w[:, (j ^ k) * feats : ((j ^ k) + 1) * feats] for j in range(4)], axis=1
            )
        )
    own_rows = rows[0]
    turned = jnp.concatenate(rows, axis=0).T
    wgrad = jnp.zeros((feats, hidden), jnp.float32)
    for start in range(0, nodes, chunk):
        here = slice(start, start + chunk)
        y = jnp.concatenate([r[:, here] for r in ys], axis=0)
        pre = jnp.dot(turned, y, preferred_element_type=jnp.float32)
        sig = jax.nn.sigmoid(pre)
        out_ref[:, here] = (pre[:feats] * sig[:feats]).astype(out_ref.dtype)
        cot = jnp.concatenate([r[:, here] for r in packed], axis=0).astype(jnp.float32)
        grad_pre = (cot * (sig * (1.0 + pre * (1.0 - sig)))).astype(jnp.bfloat16)
        grad_ref[:, here] = jnp.dot(
            own_rows, grad_pre, preferred_element_type=jnp.float32
        ).astype(grad_ref.dtype)
        wgrad += lax.dot_general(
            ys[0][:, here], grad_pre, (((1,), (1,)), ((), ())), preferred_element_type=jnp.float32
        )
    wgrad_ref[...] = exchanged_columns(wgrad, place_ref[0]) * factor


def middle(place, ys, packed):
    feats, nodes = ys[0].shape
    factor = 1.0 / math.sqrt(nodes * lax.axis_size("blk"))
    return pl.pallas_call(
        functools.partial(middle_body, factor),
        out_shape=(
            jax.ShapeDtypeStruct((feats, nodes), jnp.bfloat16),
            pltpu.VMEM((feats, nodes), jnp.bfloat16),
            pltpu.VMEM((feats, 4 * feats), jnp.float32),
        ),
        in_specs=[SMEM] + [VMEM] * 8,
        out_specs=(VMEM,) * 3,
        cost_estimate=COST,
        compiler_params=kept(10),
        name="middle",
    )(place.astype(jnp.int32).reshape(1), *map(near, ys), *map(near, packed))


def fenced(*groups):
    return lax.optimization_barrier(groups)


def per_device(x_t, weight, cotangent, tile_row, tile_col, tile_off, tile_vals, tile_count):
    nodes = x_t.shape[1]
    f32, bf16 = jnp.float32, jnp.bfloat16
    place = lax.axis_index("feat")
    sign = (1 - 2 * (lax.axis_index("blk") % 2)).astype(jnp.int32).reshape(1)
    own = jnp.concatenate([cotangent, exchanged_columns(weight, place)], axis=1)

    x, u, v = flipped(x_t, "blk", 1), stepped(x_t, True), stepped(x_t, False)
    listed = plan(tile_row, tile_col, tile_off, tile_count, sign)
    x, u, v, listed, own = fenced(x, u, v, listed, own)
    m, n, far = stepped(u, True), stepped(v, False), flipped(own, "feat", 2)
    y = forward(0, listed, tile_vals, [x_t, u, v], None, f32)
    m, n, y, x = fenced(m, n, y, x)
    mx, xu, xv = flipped(m, "blk", 1), stepped(x, True), stepped(x, False)
    y = forward(1, listed, tile_vals, [x, m, n], y, f32)
    xu, xv, mx, y, far, own = fenced(xu, xv, mx, y, far, own)
    packed = [own, flipped(own, "feat", 1), far, flipped(far, "feat", 1)]
    y = forward(2, listed, tile_vals, [xu, xv, mx], y, bf16)
    y_far = flipped(y, "feat", 2)
    ys = [y, flipped(y, "feat", 1), y_far, flipped(y_far, "feat", 1)]
    out_t, grad, wgrad = middle(place, ys, packed)

    part = flipped(wgrad, "blk", 2)
    to_xu, to_xv, to_mx = backward(2, listed, tile_vals, grad, [bf16] * 3)
    to_xu, to_xv, to_mx, part, grad = fenced(to_xu, to_xv, to_mx, part, grad)
    from_mx, from_xu, from_xv = flipped(to_mx, "blk", 1), stepped(to_xu, False), stepped(to_xv, True)
    wgrad = wgrad + part
    part = flipped(wgrad, "blk", 8)
    to_x, to_m, to_n = backward(1, listed, tile_vals, grad, [f32, f32, bf16])
    part, to_m, grad = fenced(part, to_m, grad)
    wgrad = wgrad + part
    part = flipped(wgrad, "blk", 16)
    total, to_u, to_v = backward(0, listed, tile_vals, grad, [f32] * 3)
    from_mx, from_xu, from_xv, to_m, to_n, total, to_x, to_u, to_v, part = fenced(
        from_mx, from_xu, from_xv, to_m, to_n, total, to_x, to_u, to_v, part
    )
    from_m = stepped((to_m + from_mx.astype(f32)).astype(bf16), False)
    from_n = stepped(to_n, True)
    to_x = (to_x + from_xu.astype(f32) + from_xv.astype(f32)).astype(bf16)
    wgrad = wgrad + part
    wgrad = wgrad + flipped(wgrad, "blk", 48)
    wgrad = wgrad + flipped(wgrad, "blk", 1)
    from_m, from_n, to_x, to_u, to_v, wgrad = fenced(from_m, from_n, to_x, to_u, to_v, wgrad)
    part = flipped(wgrad, "blk", 6)
    from_u = stepped((to_u + from_m.astype(f32)).astype(bf16), False)
    from_v = stepped((to_v + from_n.astype(f32)).astype(bf16), True)
    from_x = flipped(to_x, "blk", 1)
    wgrad = wgrad + part
    total = total + from_u.astype(f32) + from_v.astype(f32) + from_x.astype(f32)
    return (out_t, total.astype(bf16), wgrad)


def solution(mesh):
    placed = (
        P("feat", "blk"),
        P("feat", None),
        P("feat", "blk"),
        P("blk"),
        P("blk"),
        P("blk"),
        P("blk", None, None),
        P("blk"),
    )
    return jax.shard_map(
        per_device,
        mesh=mesh,
        in_specs=placed,
        out_specs=(P("feat", "blk"), P("feat", "blk"), P("feat", None)),
        check_vma=False,
    )
```
